512 devices in a mesh: seq: 64 (over x, y, core), ch: 8 (over z).
Axes of the slice: x: 4, y: 8, z: 8, core: 2. Of those that a mesh axis runs over, the one named last changes fastest.
Arguments:
- signal: bfloat16 [256, 32768], P('ch', 'seq'), may hold values from -6 to 6
- in_gate: bfloat16 [256, 32768], P('ch', 'seq'), may hold values from -6 to 6
- out_gate: bfloat16 [256, 32768], P('ch', 'seq'), may hold values from -6 to 6
- short_taps: float32 [256, 128], P('ch'), may hold values from -0.5 to 0.5
- skip_gain: float32 [256], P('ch'), may hold values from 0.5 to 1.5
- decay_rate: float32 [256], P('ch'), may hold values from 9.368896e-05 to 0.00046844484
- embed_weight: float32 [33, 64], replicated, may hold values from -1 to 1
- embed_bias: float32 [64], replicated, may hold values from -3.140625 to 3.140625
- sine_freq: float32 [64], replicated, may hold values from 1 to 10
- mid_weight: float32 [64, 64], replicated, may hold values from -0.75 to 0.75
- mid_bias: float32 [64], replicated, may hold values from -3.140625 to 3.140625
- out_weight: float32 [64, 256], P(None, 'ch'), may hold values from -0.75 to 0.75
Outputs:
- mixed: bfloat16 [256, 32768], P('ch', 'seq')
The draws below stay inside these ranges and needn't reach their ends.
All inputs are finite; a program needn't handle non-finite values.
Results may differ from the reference program's by a relative error of at most 0.001.
Values may be sent and summed in bfloat16 or wider, within the bound.
A program may use at most 64 MiB of HBM per device.

```python
import math
import jax
import jax.numpy as jnp
from jax import lax

C = 256
F = 64
BANDS = 16
TAPS = 128
L = 32768
EMBED = 33


def block_scale(key, shape, cuts, least, high):
    def one(axis_at, blocks):
        draws = jax.random.uniform(jax.random.fold_in(jax.random.fold_in(key, 6), axis_at), (blocks,), jnp.float32, least / len(cuts), high / len(cuts))
        return jnp.repeat(jnp.exp(draws), shape[axis_at] // blocks).reshape((-1,) + (1,) * (len(shape) - axis_at - 1))

    level = one(*cuts[0])
    for cut in cuts[1:]:
        level = level * one(*cut)
    return level


def centred(stream_key, shape, width, limit, cuts=(), held_as=jnp.bfloat16):
    factor_of = block_scale(stream_key, shape, cuts, -0.22, 0.18) if cuts else 1.0
    array = jax.random.normal(stream_key, shape, jnp.float32) * width * factor_of
    return jnp.minimum(jnp.maximum(array, -limit), limit).astype(held_as)


def setup_inputs(seed: int = 0) -> dict:
    splits = jax.random.split(jax.random.key(seed), 13)
    return {
        "signal": centred(splits[0], (C, L), 1.0, 6.0, ((0, 8), (1, 64))),
        "in_gate": centred(splits[1], (C, L), 1.0, 6.0, ((0, 8), (1, 64))),
        "out_gate": centred(splits[2], (C, L), 1.0, 6.0, ((0, 8), (1, 64))),
        "short_taps": centred(splits[3], (C, TAPS), TAPS ** -0.5, 0.5, ((0, 8),), jnp.float32),
        "skip_gain": jnp.clip(0.5 + 1.0 * jax.random.uniform(splits[4], (C,), jnp.float32) ** block_scale(splits[4], (C,), ((0, 8),), -0.2, 0.2), 0.5, 1.5),
        "decay_rate": jnp.clip(jnp.exp(math.log(0.00046844484) - 1.609438 * jax.random.uniform(splits[5], (C,), jnp.float32) ** block_scale(splits[5], (C,), ((0, 8),), -0.2, 0.2)), 9.368896280648187e-05, 0.00046844484),
        "embed_weight": centred(splits[6], (EMBED, F), EMBED ** -0.5, 1.0, (), jnp.float32),
        "embed_bias": jnp.clip(jax.random.uniform(splits[7], (F,), jnp.float32, -3.140625, 3.140625), -3.140625, 3.140625),
        "sine_freq": jnp.clip(jnp.exp(jax.random.uniform(splits[8], (F,), jnp.float32, math.log(1.0), math.log(10.0))), 1.0, 10.0),
        "mid_weight": centred(splits[9], (F, F), F ** -0.5, 0.75, (), jnp.float32),
        "mid_bias": jnp.clip(jax.random.uniform(splits[10], (F,), jnp.float32, -3.140625, 3.140625), -3.140625, 3.140625),
        "out_weight": centred(splits[11], (F, C), F ** -0.5, 0.75, ((1, 8),), jnp.float32),
    }


def embed_rows(positions, full_len):
    phase = positions % full_len
    columns = [positions.astype(jnp.float32) / full_len]
    for band in range(BANDS):
        angle = phase.astype(jnp.float32) * (2.0 * math.pi / full_len)
        columns.append(jnp.cos(angle))
        columns.append(jnp.sin(angle))
        phase = 2 * phase % full_len
    return jnp.stack(columns, axis=1)

def filter_hidden(positions, full_len, embed_weight, embed_bias, sine_freq, mid_weight, mid_bias):
    embedding = embed_rows(positions, full_len)
    first = jnp.sin(sine_freq * (jnp.dot(embedding, embed_weight, precision=lax.Precision.HIGHEST, preferred_element_type=jnp.float32) + embed_bias))
    return jnp.sin(sine_freq * (jnp.dot(first, mid_weight, precision=lax.Precision.HIGHEST, preferred_element_type=jnp.float32) + mid_bias))

def shape_filter(second, positions, out_weight, decay_rate):
    raw_vals = jnp.dot(second, out_weight, precision=lax.Precision.HIGHEST, preferred_element_type=jnp.float32).T
    return raw_vals * (jnp.sqrt(2.0 * decay_rate)[:, None] * jnp.exp(-decay_rate[:, None] * positions.astype(jnp.float32)[None, :]))

def reference(signal, in_gate, out_gate, short_taps, skip_gain, decay_rate, embed_weight, embed_bias, sine_freq, mid_weight, mid_bias, out_weight):
    channels, full_len = signal.shape
    tap_count = short_taps.shape[1]
    values = signal.astype(jnp.float32)
    padded = jnp.pad(values, ((0, 0), (tap_count - 1, 0)))
    short_out = jnp.zeros_like(values)
    for lag in range(tap_count):
        begin = tap_count - 1 - lag
        short_out = short_out + short_taps[:, lag:lag + 1] * padded[:, begin:begin + full_len]
    gated_in = in_gate.astype(jnp.float32) * short_out
    positions = jnp.arange(full_len, dtype=jnp.int32)
    second = filter_hidden(positions, full_len, embed_weight, embed_bias, sine_freq, mid_weight, mid_bias)
    filter_vals = shape_filter(second, positions, out_weight, decay_rate)
    fft_len = 2 * full_len
    spectrum = jnp.fft.rfft(gated_in, n=fft_len, axis=1) * jnp.fft.rfft(filter_vals, n=fft_len, axis=1)
    conv = jnp.fft.irfft(spectrum, n=fft_len, axis=1)[:, :full_len]
    return (out_gate.astype(jnp.float32) * (conv + skip_gain[:, None] * gated_in)).astype(jnp.bfloat16)
```

```python
import functools
import math

import jax
import jax.numpy as jnp
import ml_dtypes
import numpy as np
from jax import lax
from jax.experimental import pallas as pl
from jax.experimental.pallas import tpu as pltpu
from jax.sharding import PartitionSpec as P

MESH = pl.DeviceIdType.MESH
HIGHEST = lax.Precision.HIGHEST
LANES = 128

SINE = (
    25.132741928100586,
    -64.83584594726562,
    67.07760620117188,
    -38.512542724609375,
    14.178224563598633,
    -3.618709087371826,
    0.6094773411750793,
)


def halves(table):
    high = table.astype(ml_dtypes.bfloat16)
    low = (table - high.astype(np.float64)).astype(ml_dtypes.bfloat16)
    return high, low


def tables(full_len):
    rows = full_len // LANES
    rows2 = 2 * rows
    k1 = np.arange(rows)[:, None] + 0.5
    angle = 2.0 * np.pi * k1 * np.arange(rows)[None, :] / rows2
    outer = np.concatenate([np.cos(angle), -np.sin(angle)], axis=0)
    turn = 2.0 * np.pi * k1 * np.arange(LANES)[None, :] / (2 * full_len)
    twiddle = np.stack([np.cos(turn), np.sin(turn)]).astype(np.float32)
    angle = 2.0 * np.pi * (np.outer(np.arange(LANES), np.arange(LANES)) % LANES) / LANES
    inner = np.block([[np.cos(angle), -np.sin(angle)], [np.sin(angle), np.cos(angle)]])
    back = outer.T * (2.0 / (2 * full_len))
    return (
        np.stack(halves(outer)),
        np.stack(halves(inner)),
        np.stack(halves(inner.T)),
        np.stack(halves(back)),
        twiddle,
    )


def sine_of_turns(turns):
    turns = turns - jnp.round(turns)
    square = turns * turns
    total = jnp.full_like(square, SINE[-1])
    for coefficient in SINE[-2::-1]:
        total = total * square + coefficient
    return total * (turns * (0.25 - square))


def split(value):
    high = value.astype(jnp.bfloat16)
    return high, (value - high.astype(jnp.float32)).astype(jnp.bfloat16)


def dot(a, b):
    return jnp.dot(a, b, preferred_element_type=jnp.float32)


def dot3(a, b):
    return dot(a[0], b[0]) + dot(a[0], b[1]) + dot(a[1], b[0])


def dot_first(a, b):
    return lax.dot_general(
        a, b, (((0,), (0,)), ((), ())), precision=HIGHEST, preferred_element_type=jnp.float32
    )


def kernel(
    seq_devs,
    signal,
    in_gate,
    taps,
    skip,
    decay,
    embed_weight,
    embed_bias,
    sine_freq,
    mid_weight,
    mid_bias,
    out_weight,
    outer_hbm,
    inner_hbm,
    inner_back_hbm,
    back_hbm,
    twiddle_hbm,
    result,
    outer,
    inner,
    inner_back,
    back,
    twiddle,
    weight1,
    weight2,
    hidden,
    packed32,
    packed,
    arrived,
    answer,
    answers,
    table_sem,
    send_sem,
    recv_sem,
    back_send_sem,
    back_recv_sem,
):
    channels, local_len = signal.shape
    units = mid_weight.shape[0]
    feats = embed_weight.shape[0]
    per_block = local_len // LANES
    full_len = seq_devs * local_len
    rows = full_len // LANES
    owners = channels
    stride = seq_devs // owners
    me = lax.axis_index("seq")
    mine = me // stride
    owner = me % stride == 0

    barrier = pltpu.get_barrier_semaphore()
    loads = [
        pltpu.make_async_copy(source, target, table_sem.at[index])
        for index, (source, target) in enumerate(
            (
                (outer_hbm, outer),
                (inner_hbm, inner),
                (inner_back_hbm, inner_back),
                (back_hbm, back),
                (twiddle_hbm, twiddle),
            )
        )
    ]

    @pl.when(owner)
    def _():
        def greet(index, carry):
            other = (me + seq_devs - 1 - index) % seq_devs
            pl.semaphore_signal(barrier, inc=1, device_id={"seq": other}, device_id_type=MESH)
            return carry

        lax.fori_loop(0, seq_devs - 1, greet, 0)
        for load in loads:
            load.start()

    row = lax.broadcasted_iota(jnp.int32, weight1.shape[:1] + (local_len,), 0)
    token = me * local_len + lax.broadcasted_iota(jnp.int32, row.shape, 1)
    band = jnp.clip((row - 1) // 2, 0, 15)
    phase = (token << band) & (full_len - 1)
    turns = phase.astype(jnp.float32) * (1.0 / full_len) + jnp.where(row % 2 == 1, 0.25, 0.0)
    place = token.astype(jnp.float32) * (1.0 / full_len)
    features = jnp.where(
        row == 0,
        place,
        jnp.where(row < feats, sine_of_turns(turns), jnp.where(row == feats, 1.0, 0.0)),
    )
    freq = sine_freq[...] * (0.5 / math.pi)
    weight1[...] = jnp.zeros_like(weight1)
    weight1[0:feats, :] = embed_weight[...] * freq
    weight1[feats : feats + 1, :] = embed_bias[...] * freq
    weight2[...] = jnp.zeros_like(weight2)
    weight2[0:units, :] = mid_weight[...] * freq
    weight2[units : units + 1, :] = mid_bias[...] * freq
    hidden[...] = jnp.where(
        lax.broadcasted_iota(jnp.int32, hidden.shape, 0) == units, 1.0, 0.0
    )
    hidden[0:units, :] = sine_of_turns(dot_first(weight1[...], features))
    second = sine_of_turns(dot_first(weight2[...], hidden[...]))
    rate = decay[...]
    raw = dot_first(out_weight[...] * jnp.sqrt(2.0 * rate), second)
    first_row = lax.broadcasted_iota(jnp.int32, (8, local_len), 0) == 0
    times = jnp.where(first_row, token[0:8, :].astype(jnp.float32), 0.0)
    rates = jnp.where(
        lax.broadcasted_iota(jnp.int32, (8, channels), 0) == 0,
        jnp.broadcast_to(rate, (8, channels)),
        0.0,
    )
    filt = raw * jnp.exp(-dot_first(rates, times))
    filt_high = filt.astype(jnp.bfloat16).astype(jnp.float32)

    parts = (
        signal[...].astype(jnp.float32),
        in_gate[...].astype(jnp.float32),
        filt_high,
        filt - filt_high,
    )
    height = len(parts) * per_block
    for kind, part in enumerate(parts):
        for quarter in range(per_block):
            packed32[pl.ds(kind * per_block + quarter, channels, stride=height), :] = part[
                :, quarter * LANES : (quarter + 1) * LANES
            ]
    packed[...] = packed32[...].astype(jnp.bfloat16).reshape(packed.shape)

    @pl.when(owner)
    def _():
        pl.semaphore_wait(barrier, owners - 1)

    @pl.when(jnp.logical_not(owner))
    def _():
        pl.semaphore_wait(barrier, owners)

    def send(index, carry):
        target = (mine + owners // 2 + index) % owners
        device = target * stride

        @pl.when(device == me)
        def _():
            pltpu.make_async_copy(packed.at[target], arrived.at[me], recv_sem).start()

        @pl.when(device != me)
        def _():
            pltpu.make_async_remote_copy(
                src_ref=packed.at[target],
                dst_ref=arrived.at[me],
                send_sem=send_sem,
                recv_sem=recv_sem,
                device_id={"seq": device},
                device_id_type=MESH,
            ).start()

        return carry

    lax.fori_loop(0, owners, send, 0)

    @pl.when(owner)
    def _():
        taps_row = jnp.broadcast_to(taps[pl.ds(mine, 1), :], (LANES, LANES))
        circulant = pltpu.roll(taps_row, 0, 1, stride=1, stride_axis=0)
        source = lax.broadcasted_iota(jnp.int32, (LANES, LANES), 0)
        target = lax.broadcasted_iota(jnp.int32, (LANES, LANES), 1)
        same = target >= source
        toeplitz = jnp.concatenate(
            [jnp.where(same, circulant, 0.0), jnp.where(same, 0.0, circulant)], axis=1
        )
        toeplitz = jnp.concatenate(split(toeplitz), axis=0)
        gain = skip[mine]
        for load in loads:
            load.wait()
        pltpu.make_async_copy(arrived, arrived, recv_sem).wait()

        blocks = arrived[...].astype(jnp.float32).reshape(seq_devs // 2, 2, height, LANES)
        upper = lax.broadcasted_iota(jnp.int32, (seq_devs // 2, 8, LANES), 1) < per_block

        def unpack(pair):
            even = blocks[:, 0, 8 * pair : 8 * pair + 8, :]
            odd = blocks[:, 1, 8 * pair : 8 * pair + 8, :]
            one = jnp.where(upper, even, pltpu.roll(odd, 4, 1))
            two = jnp.where(upper, pltpu.roll(even, 4, 1), odd)
            return one.reshape(rows, LANES), two.reshape(rows, LANES)

        values, gates = unpack(0)
        filter_parts = [part.astype(jnp.bfloat16) for part in unpack(1)]
        values = values.astype(jnp.bfloat16)
        both = dot(jnp.concatenate([values, values], axis=1), toeplitz)
        later = pltpu.roll(both[:, LANES:], 1, 0)
        later = jnp.where(lax.broadcasted_iota(jnp.int32, later.shape, 0) == 0, 0.0, later)
        gated = gates * (both[:, :LANES] + later)

        gated_parts = split(gated)
        columns = [
            jnp.concatenate([g, f], axis=1) for g, f in zip(gated_parts, filter_parts)
        ]
        outer_cols = dot3((outer[0], outer[1]), columns)
        real, imag = outer_cols[:rows, :], outer_cols[rows:, :]
        cosine = jnp.concatenate([twiddle[0], twiddle[0]], axis=1)
        sine = jnp.concatenate([twiddle[1], twiddle[1]], axis=1)
        turned_real = real * cosine + imag * sine
        turned_imag = imag * cosine - real * sine

        def spectrum(lanes):
            joined = jnp.concatenate([turned_real[:, lanes], turned_imag[:, lanes]], axis=1)
            full = dot3(split(joined), (inner[0], inner[1]))
            return full[:, :LANES], full[:, LANES:]

        gated_real, gated_imag = spectrum(slice(0, LANES))
        filt_real, filt_imag = spectrum(slice(LANES, 2 * LANES))
        product = jnp.concatenate(
            [
                gated_real * filt_real - gated_imag * filt_imag,
                gated_real * filt_imag + gated_imag * filt_real,
            ],
            axis=1,
        )
        undone = dot3(split(product), (inner_back[0], inner_back[1]))
        real, imag = undone[:, :LANES], undone[:, LANES:]
        cosine, sine = twiddle[0], twiddle[1]
        stacked = jnp.concatenate(
            [real * cosine - imag * sine, imag * cosine + real * sine], axis=0
        )
        conv = dot3((back[0], back[1]), split(stacked))
        answer[...] = (conv + gain * gated).reshape(answer.shape)

        def reply(index, carry):
            device = (me + seq_devs // 2 + index) % seq_devs

            @pl.when(device == me)
            def _():
                pltpu.make_async_copy(
                    answer.at[device], answers.at[mine], back_recv_sem
                ).start()

            @pl.when(device != me)
            def _():
                pltpu.make_async_remote_copy(
                    src_ref=answer.at[device],
                    dst_ref=answers.at[mine],
                    send_sem=back_send_sem,
                    recv_sem=back_recv_sem,
                    device_id={"seq": device},
                    device_id_type=MESH,
                ).start()

            return carry

        lax.fori_loop(0, seq_devs, reply, 0)

    pltpu.make_async_copy(answers, answers, back_recv_sem).wait()
    for quarter in range(per_block):
        result[:, quarter * LANES : (quarter + 1) * LANES] = answers[:, quarter, :]

    @pl.when(owner)
    def _():
        sent = packed.at[0 : owners - 1]
        pltpu.make_async_copy(sent, sent, send_sem).wait()
        replied = answer.at[0 : seq_devs - 1]
        pltpu.make_async_copy(replied, replied, back_send_sem).wait()

    @pl.when(jnp.logical_not(owner))
    def _():
        pltpu.make_async_copy(packed, packed, send_sem).wait()


def on_device(
    consts,
    signal,
    in_gate,
    out_gate,
    short_taps,
    skip_gain,
    decay_rate,
    embed_weight,
    embed_bias,
    sine_freq,
    mid_weight,
    mid_bias,
    out_weight,
):
    channels, local_len = signal.shape
    seq_devs = lax.axis_size("seq")
    rows = seq_devs * local_len // LANES
    per_block = local_len // LANES
    units = mid_weight.shape[0]
    vmem = pl.BlockSpec(memory_space=pltpu.VMEM)
    smem = pl.BlockSpec(memory_space=pltpu.SMEM)
    hbm = pl.BlockSpec(memory_space=pl.ANY)
    height1 = (embed_weight.shape[0] + 1 + 7) // 8 * 8
    height2 = (units + 1 + 7) // 8 * 8
    result = pl.pallas_call(
        functools.partial(kernel, seq_devs),
        out_shape=jax.ShapeDtypeStruct((channels, local_len), jnp.float32),
        in_specs=[vmem, vmem, vmem, smem] + [vmem] * 7 + [hbm] * 5,
        out_specs=vmem,
        scratch_shapes=[
            *[pltpu.VMEM(const.shape, const.dtype) for const in consts],
            pltpu.VMEM((height1, units), jnp.float32),
            pltpu.VMEM((height2, units), jnp.float32),
            pltpu.VMEM((height2, local_len), jnp.float32),
            pltpu.VMEM((channels * 4 * per_block, LANES), jnp.float32),
            pltpu.VMEM((channels, 4 * per_block, LANES), jnp.bfloat16),
            pltpu.VMEM((seq_devs, 4 * per_block, LANES), jnp.bfloat16),
            pltpu.VMEM((seq_devs, per_block, LANES), jnp.float32),
            pltpu.VMEM((channels, per_block, LANES), jnp.float32),
            pltpu.SemaphoreType.DMA((5,)),
            pltpu.SemaphoreType.DMA,
            pltpu.SemaphoreType.DMA,
            pltpu.SemaphoreType.DMA,
            pltpu.SemaphoreType.DMA,
        ],
        compiler_params=pltpu.CompilerParams(collective_id=0, has_side_effects=True),
    )(
        signal,
        in_gate,
        short_taps,
        skip_gain,
        decay_rate[None, :],
        embed_weight,
        embed_bias[None, :],
        sine_freq[None, :],
        mid_weight,
        mid_bias[None, :],
        out_weight,
        *[jnp.asarray(const) for const in consts],
    )
    return (out_gate.astype(jnp.float32) * result).astype(jnp.bfloat16)


def solution(mesh):
    consts = tables(32768)
    in_specs = (
        P("ch", "seq"),
        P("ch", "seq"),
        P("ch", "seq"),
        P("ch", None),
        P("ch"),
        P("ch"),
        P(),
        P(),
        P(),
        P(),
        P(),
        P(None, "ch"),
    )
    return jax.shard_map(
        functools.partial(on_device, consts),
        mesh=mesh,
        in_specs=in_specs,
        out_specs=P("ch", "seq"),
        check_vma=False,
    )
```

```python
import functools
import math

import jax
import jax.numpy as jnp
import ml_dtypes
import numpy as np
from jax import lax
from jax.experimental import pallas as pl
from jax.experimental.pallas import tpu as pltpu
from jax.sharding import PartitionSpec as P

MESH = pl.DeviceIdType.MESH
HIGHEST = lax.Precision.HIGHEST
LANES = 128

SINE = (
    25.132741928100586,
    -64.83584594726562,
    67.07760620117188,
    -38.512542724609375,
    14.178224563598633,
    -3.618709087371826,
    0.6094773411750793,
)


def halves(table):
    high = table.astype(ml_dtypes.bfloat16)
    low = (table - high.astype(np.float64)).astype(ml_dtypes.bfloat16)
    return high, low


def tables(full_len):
    rows = full_len // LANES
    rows2 = 2 * rows
    k1 = np.arange(rows)[:, None] + 0.5
    angle = 2.0 * np.pi * k1 * np.arange(rows)[None, :] / rows2
    outer = np.concatenate([np.cos(angle), -np.sin(angle)], axis=0)
    turn = 2.0 * np.pi * k1 * np.arange(LANES)[None, :] / (2 * full_len)
    twiddle = np.stack([np.cos(turn), np.sin(turn)]).astype(np.float32)
    angle = 2.0 * np.pi * (np.outer(np.arange(LANES), np.arange(LANES)) % LANES) / LANES
    inner = np.block([[np.cos(angle), -np.sin(angle)], [np.sin(angle), np.cos(angle)]])
    back = outer.T * (2.0 / (2 * full_len))
    return (
        np.stack(halves(outer)),
        np.stack(halves(inner)),
        np.stack(halves(inner.T)),
        np.stack(halves(back)),
        twiddle,
    )


def sine_of_turns(turns):
    turns = turns - jnp.round(turns)
    square = turns * turns
    total = jnp.full_like(square, SINE[-1])
    for coefficient in SINE[-2::-1]:
        total = total * square + coefficient
    return total * (turns * (0.25 - square))


def split(value):
    high = value.astype(jnp.bfloat16)
    return high, (value - high.astype(jnp.float32)).astype(jnp.bfloat16)


def dot(a, b):
    return jnp.dot(a, b, preferred_element_type=jnp.float32)


def dot3(a, b):
    return dot(a[0], b[0]) + dot(a[0], b[1]) + dot(a[1], b[0])


def dot_first(a, b, axis=0):
    return lax.dot_general(
        a, b, (((axis,), (0,)), ((), ())), precision=HIGHEST, preferred_element_type=jnp.float32
    )


def kernel(
    seq_devs,
    *refs,
):
    sources, refs = refs[:16], refs[16:]
    result, targets, refs = refs[0], refs[1:17], refs[17:]
    signal, in_gate, taps, skip, decay = targets[:5]
    embed_weight, embed_bias, sine_freq, mid_weight, mid_bias, out_weight = targets[5:11]
    outer, inner, inner_back, back, twiddle = targets[11:]
    weight1, weight2, hidden, packed32, packed, arrived, answer, answers = refs[:8]
    load_sem, send_sem, recv_sem, back_send_sem, back_recv_sem = refs[8:]
    channels, local_len = signal.shape
    units = mid_weight.shape[0]
    feats = embed_weight.shape[0]
    per_block = local_len // LANES
    full_len = seq_devs * local_len
    rows = full_len // LANES
    owners = channels
    stride = seq_devs // owners
    me = lax.axis_index("seq")
    mine = me // stride
    owner = me % stride == 0

    barrier = pltpu.get_barrier_semaphore()
    loads = [
        pltpu.make_async_copy(source, target, load_sem.at[index])
        for index, (source, target) in enumerate(zip(sources, targets))
    ]
    first_loads, weight_loads, owner_loads = loads[:2], loads[4:11], loads[2:4] + loads[11:]

    @pl.when(owner)
    def _():
        def greet(index, carry):
            other = (me + seq_devs - 1 - index) % seq_devs
            pl.semaphore_signal(barrier, inc=1, device_id={"seq": other}, device_id_type=MESH)
            return carry

        lax.fori_loop(0, seq_devs - 1, greet, 0)

    for load in weight_loads + first_loads:
        load.start()

    @pl.when(owner)
    def _():
        for load in owner_loads:
            load.start()

    row = lax.broadcasted_iota(jnp.int32, weight1.shape[:1] + (local_len,), 0)
    token = me * local_len + lax.broadcasted_iota(jnp.int32, row.shape, 1)
    band = jnp.clip((row - 1) // 2, 0, 15)
    phase = (token << band) & (full_len - 1)
    turns = phase.astype(jnp.float32) * (1.0 / full_len) + jnp.where(row % 2 == 1, 0.25, 0.0)
    place = token.astype(jnp.float32) * (1.0 / full_len)
    features = jnp.where(
        row == 0,
        place,
        jnp.where(row < feats, sine_of_turns(turns), jnp.where(row == feats, 1.0, 0.0)),
    )
    for load in weight_loads:
        load.wait()
    freq = sine_freq[...] * (0.5 / math.pi)
    weight1[...] = jnp.zeros_like(weight1)
    weight1[0:feats, :] = embed_weight[...] * freq
    weight1[feats : feats + 1, :] = embed_bias[...] * freq
    weight2[...] = jnp.zeros_like(weight2)
    weight2[0:units, :] = mid_weight[...] * freq
    weight2[units : units + 1, :] = mid_bias[...] * freq
    hidden[...] = jnp.where(
        lax.broadcasted_iota(jnp.int32, hidden.shape, 0) == units, 1.0, 0.0
    )
    hidden[0:units, :] = sine_of_turns(dot_first(weight1[...], features))
    second = sine_of_turns(dot_first(weight2[...], hidden[...]))
    rate = decay[...]
    raw = dot_first(out_weight[...], second, 1)
    row = lax.broadcasted_iota(jnp.int32, (8, channels), 0)
    rates = jnp.broadcast_to(rate, row.shape)
    rates = jnp.where(row == 0, -rates, jnp.where(row == 1, 0.5 * jnp.log(2.0 * rates), 0.0))
    row = lax.broadcasted_iota(jnp.int32, (8, local_len), 0)
    times = jnp.where(row == 0, token[0:8, :].astype(jnp.float32), jnp.where(row == 1, 1.0, 0.0))
    filt = raw * jnp.exp(dot_first(rates, times))
    filt_high = filt.astype(jnp.bfloat16).astype(jnp.float32)

    for load in first_loads:
        load.wait()

    parts = (
        signal[...].astype(jnp.float32),
        in_gate[...].astype(jnp.float32),
        filt_high,
        filt - filt_high,
    )
    height = len(parts) * per_block
    for kind, part in enumerate(parts):
        for quarter in range(per_block):
            packed32[pl.ds(kind * per_block + quarter, channels, stride=height), :] = part[
                :, quarter * LANES : (quarter + 1) * LANES
            ]
    packed[...] = packed32[...].astype(jnp.bfloat16).reshape(packed.shape)

    @pl.when(owner)
    def _():
        pl.semaphore_wait(barrier, owners - 1)

    @pl.when(jnp.logical_not(owner))
    def _():
        pl.semaphore_wait(barrier, owners)

    def send(index, carry):
        target = (mine + owners // 2 + index) % owners
        device = target * stride

        @pl.when(device == me)
        def _():
            pltpu.make_async_copy(packed.at[target], arrived.at[me], recv_sem).start()

        @pl.when(device != me)
        def _():
            pltpu.make_async_remote_copy(
                src_ref=packed.at[target],
                dst_ref=arrived.at[me],
                send_sem=send_sem,
                recv_sem=recv_sem,
                device_id={"seq": device},
                device_id_type=MESH,
            ).start()

        return carry

    lax.fori_loop(0, owners, send, 0)

    @pl.when(owner)
    def _():
        for load in owner_loads:
            load.wait()

        taps_row = jnp.broadcast_to(taps[pl.ds(mine, 1), :], (LANES, LANES))
        circulant = pltpu.roll(taps_row, 0, 1, stride=1, stride_axis=0)
        source = lax.broadcasted_iota(jnp.int32, (LANES, LANES), 0)
        target = lax.broadcasted_iota(jnp.int32, (LANES, LANES), 1)
        same = target >= source
        toeplitz = jnp.concatenate(
            [jnp.where(same, circulant, 0.0), jnp.where(same, 0.0, circulant)], axis=1
        )
        toeplitz = jnp.concatenate(split(toeplitz), axis=0)
        lane = lax.broadcasted_iota(jnp.int32, (1, channels), 1)
        gain = jnp.sum(jnp.where(lane == mine, skip[...], 0.0), axis=1, keepdims=True)
        pltpu.make_async_copy(arrived, arrived, recv_sem).wait()

        blocks = arrived[...].astype(jnp.float32).reshape(seq_devs // 2, 2, height, LANES)
        upper = lax.broadcasted_iota(jnp.int32, (seq_devs // 2, 8, LANES), 1) < per_block

        def unpack(pair):
            even = blocks[:, 0, 8 * pair : 8 * pair + 8, :]
            odd = blocks[:, 1, 8 * pair : 8 * pair + 8, :]
            one = jnp.where(upper, even, pltpu.roll(odd, 4, 1))
            two = jnp.where(upper, pltpu.roll(even, 4, 1), odd)
            return one.reshape(rows, LANES), two.reshape(rows, LANES)

        values, gates = unpack(0)
        filter_parts = [part.astype(jnp.bfloat16) for part in unpack(1)]
        values = values.astype(jnp.bfloat16)
        both = dot(jnp.concatenate([values, values], axis=1), toeplitz)
        later = pltpu.roll(both[:, LANES:], 1, 0)
        later = jnp.where(lax.broadcasted_iota(jnp.int32, later.shape, 0) == 0, 0.0, later)
        gated = gates * (both[:, :LANES] + later)

        gated_parts = split(gated)
        columns = [
            jnp.concatenate([g, f], axis=1) for g, f in zip(gated_parts, filter_parts)
        ]
        outer_cols = dot3((outer[0], outer[1]), columns)
        real, imag = outer_cols[:rows, :], outer_cols[rows:, :]
        cosine = jnp.concatenate([twiddle[0], twiddle[0]], axis=1)
        sine = jnp.concatenate([twiddle[1], twiddle[1]], axis=1)
        turned_real = real * cosine + imag * sine
        turned_imag = imag * cosine - real * sine

        def spectrum(lanes):
            joined = jnp.concatenate([turned_real[:, lanes], turned_imag[:, lanes]], axis=1)
            full = dot3(split(joined), (inner[0], inner[1]))
            return full[:, :LANES], full[:, LANES:]

        gated_real, gated_imag = spectrum(slice(0, LANES))
        filt_real, filt_imag = spectrum(slice(LANES, 2 * LANES))
        product = jnp.concatenate(
            [
                gated_real * filt_real - gated_imag * filt_imag,
                gated_real * filt_imag + gated_imag * filt_real,
            ],
            axis=1,
        )
        undone = dot3(split(product), (inner_back[0], inner_back[1]))
        real, imag = undone[:, :LANES], undone[:, LANES:]
        cosine, sine = twiddle[0], twiddle[1]
        stacked = jnp.concatenate(
            [real * cosine - imag * sine, imag * cosine + real * sine], axis=0
        )
        conv = dot3((back[0], back[1]), split(stacked))
        answer[...] = (conv + gain * gated).reshape(answer.shape)

        def reply(index, carry):
            device = (me + seq_devs // 2 + index) % seq_devs

            @pl.when(device == me)
            def _():
                pltpu.make_async_copy(
                    answer.at[device], answers.at[mine], back_recv_sem
                ).start()

            @pl.when(device != me)
            def _():
                pltpu.make_async_remote_copy(
                    src_ref=answer.at[device],
                    dst_ref=answers.at[mine],
                    send_sem=back_send_sem,
                    recv_sem=back_recv_sem,
                    device_id={"seq": device},
                    device_id_type=MESH,
                ).start()

            return carry

        lax.fori_loop(0, seq_devs, reply, 0)

    pltpu.make_async_copy(answers, answers, back_recv_sem).wait()
    for quarter in range(per_block):
        result[:, quarter * LANES : (quarter + 1) * LANES] = answers[:, quarter, :]

    @pl.when(owner)
    def _():
        sent = packed.at[0 : owners - 1]
        pltpu.make_async_copy(sent, sent, send_sem).wait()
        replied = answer.at[0 : seq_devs - 1]
        pltpu.make_async_copy(replied, replied, back_send_sem).wait()

    @pl.when(jnp.logical_not(owner))
    def _():
        pltpu.make_async_copy(packed, packed, send_sem).wait()


def on_device(
    consts,
    signal,
    in_gate,
    out_gate,
    short_taps,
    skip_gain,
    decay_rate,
    embed_weight,
    embed_bias,
    sine_freq,
    mid_weight,
    mid_bias,
    out_weight,
):
    channels, local_len = signal.shape
    seq_devs = lax.axis_size("seq")
    per_block = local_len // LANES
    units = mid_weight.shape[0]
    vmem = pl.BlockSpec(memory_space=pltpu.VMEM)
    operands = (
        signal,
        in_gate,
        short_taps,
        skip_gain[None, :],
        decay_rate[None, :],
        embed_weight,
        embed_bias[None, :],
        sine_freq[None, :],
        mid_weight,
        mid_bias[None, :],
        out_weight.T,
        *[jnp.asarray(const) for const in consts],
    )
    height1 = (embed_weight.shape[0] + 1 + 7) // 8 * 8
    height2 = (units + 1 + 7) // 8 * 8
    result = pl.pallas_call(
        functools.partial(kernel, seq_devs),
        out_shape=pltpu.VMEM((channels, local_len), jnp.float32),
        in_specs=[pl.BlockSpec(memory_space=pl.ANY)] * len(operands),
        out_specs=vmem,
        scratch_shapes=[
            *[pltpu.VMEM(operand.shape, operand.dtype) for operand in operands],
            pltpu.VMEM((height1, units), jnp.float32),
            pltpu.VMEM((height2, units), jnp.float32),
            pltpu.VMEM((height2, local_len), jnp.float32),
            pltpu.VMEM((channels * 4 * per_block, LANES), jnp.float32),
            pltpu.VMEM((channels, 4 * per_block, LANES), jnp.bfloat16),
            pltpu.VMEM((seq_devs, 4 * per_block, LANES), jnp.bfloat16),
            pltpu.VMEM((seq_devs, per_block, LANES), jnp.float32),
            pltpu.VMEM((channels, per_block, LANES), jnp.float32),
            pltpu.SemaphoreType.DMA((len(operands),)),
            pltpu.SemaphoreType.DMA,
            pltpu.SemaphoreType.DMA,
            pltpu.SemaphoreType.DMA,
            pltpu.SemaphoreType.DMA,
        ],
        compiler_params=pltpu.CompilerParams(collective_id=0, has_side_effects=True),
    )(*operands)
    return (out_gate.astype(jnp.float32) * result).astype(jnp.bfloat16)


def solution(mesh):
    consts = tables(32768)
    in_specs = (
        P("ch", "seq"),
        P("ch", "seq"),
        P("ch", "seq"),
        P("ch", None),
        P("ch"),
        P("ch"),
        P(),
        P(),
        P(),
        P(),
        P(),
        P(None, "ch"),
    )
    return jax.shard_map(
        functools.partial(on_device, consts),
        mesh=mesh,
        in_specs=in_specs,
        out_specs=P("ch", "seq"),
        check_vma=False,
    )
```

```python
import functools
import math

import jax
import jax.numpy as jnp
import ml_dtypes
import numpy as np
from jax import lax
from jax.experimental import pallas as pl
from jax.experimental.pallas import tpu as pltpu
from jax.sharding import PartitionSpec as P

MESH = pl.DeviceIdType.MESH
HIGHEST = lax.Precision.HIGHEST
LANES = 128
GRID = (4, 8)
CORES = 2

SINE = (
    25.132741928100586,
    -64.83584594726562,
    67.07760620117188,
    -38.512542724609375,
    14.178224563598633,
    -3.618709087371826,
    0.6094773411750793,
)


def far_first():
    def hops(offset):
        return sum(min(step, size - step) for step, size in zip(offset, GRID))

    offsets = [(dx, dy) for dx in range(GRID[0]) for dy in range(GRID[1])]
    return sorted(offsets, key=hops, reverse=True)


def halves(table):
    high = table.astype(ml_dtypes.bfloat16)
    low = (table - high.astype(np.float64)).astype(ml_dtypes.bfloat16)
    return high, low


def tables(full_len):
    rows = full_len // LANES
    rows2 = 2 * rows
    k1 = np.arange(rows)[:, None] + 0.5
    angle = 2.0 * np.pi * k1 * np.arange(rows)[None, :] / rows2
    outer = np.concatenate([np.cos(angle), -np.sin(angle)], axis=0)
    turn = 2.0 * np.pi * k1 * np.arange(LANES)[None, :] / (2 * full_len)
    twiddle = np.stack([np.cos(turn), np.sin(turn)]).astype(np.float32)
    angle = 2.0 * np.pi * (np.outer(np.arange(LANES), np.arange(LANES)) % LANES) / LANES
    inner = np.block([[np.cos(angle), -np.sin(angle)], [np.sin(angle), np.cos(angle)]])
    back = outer.T * (2.0 / (2 * full_len))
    return (
        np.stack(halves(outer)),
        np.stack(halves(inner)),
        np.stack(halves(inner.T)),
        np.stack(halves(back)),
        twiddle,
    )


def sine_of_turns(turns):
    turns = turns - jnp.round(turns)
    square = turns * turns
    total = jnp.full_like(square, SINE[-1])
    for coefficient in SINE[-2::-1]:
        total = total * square + coefficient
    return total * (turns * (0.25 - square))


def split(value):
    high = value.astype(jnp.bfloat16)
    return high, (value - high.astype(jnp.float32)).astype(jnp.bfloat16)


def dot(a, b):
    return jnp.dot(a, b, preferred_element_type=jnp.float32)


def dot3(a, b):
    return dot(a[0], b[0]) + dot(a[0], b[1]) + dot(a[1], b[0])


def dot_first(a, b, axis=0):
    return lax.dot_general(
        a, b, (((axis,), (0,)), ((), ())), precision=HIGHEST, preferred_element_type=jnp.float32
    )


def kernel(
    seq_devs,
    *refs,
):
    sources, refs = refs[:16], refs[16:]
    result, targets, refs = refs[0], refs[1:17], refs[17:]
    signal, in_gate, taps, skip, decay = targets[:5]
    embed_weight, embed_bias, sine_freq, mid_weight, mid_bias, out_weight = targets[5:11]
    outer, inner, inner_back, back, twiddle = targets[11:]
    weight1, weight2, hidden, packed32, packed, arrived, answer, answers = refs[:8]
    load_sem, send_sem, recv_sem, back_send_sem, back_recv_sem = refs[8:]
    channels, local_len = signal.shape
    units = mid_weight.shape[0]
    feats = embed_weight.shape[0]
    per_block = local_len // LANES
    full_len = seq_devs * local_len
    rows = full_len // LANES
    owners = channels
    me = lax.axis_index("seq")
    mine = me // CORES
    owner = me % CORES == 0
    by_x = [(mine // GRID[1] + dx) % GRID[0] * GRID[1] for dx in range(GRID[0])]
    by_y = [(mine % GRID[1] + dy) % GRID[1] for dy in range(GRID[1])]
    chips = [(by_x[dx] + by_y[dy], dx == dy == 0) for dx, dy in far_first()]

    barrier = pltpu.get_barrier_semaphore()
    loads = [
        pltpu.make_async_copy(source, target, load_sem.at[index])
        for index, (source, target) in enumerate(zip(sources, targets))
    ]
    first_loads, weight_loads, owner_loads = loads[:2], loads[4:11], loads[2:4] + loads[11:]

    @pl.when(owner)
    def _():
        for chip, here in chips:
            for core in range(1 if here else 0, CORES):
                pl.semaphore_signal(
                    barrier,
                    inc=1,
                    device_id={"seq": chip * CORES + core},
                    device_id_type=MESH,
                )

    for load in weight_loads + first_loads:
        load.start()

    @pl.when(owner)
    def _():
        for load in owner_loads:
            load.start()

    row = lax.broadcasted_iota(jnp.int32, weight1.shape[:1] + (local_len,), 0)
    token = me * local_len + lax.broadcasted_iota(jnp.int32, row.shape, 1)
    band = jnp.clip((row - 1) // 2, 0, 15)
    phase = (token << band) & (full_len - 1)
    turns = phase.astype(jnp.float32) * (1.0 / full_len) + jnp.where(row % 2 == 1, 0.25, 0.0)
    place = token.astype(jnp.float32) * (1.0 / full_len)
    features = jnp.where(
        row == 0,
        place,
        jnp.where(row < feats, sine_of_turns(turns), jnp.where(row == feats, 1.0, 0.0)),
    )
    for load in weight_loads:
        load.wait()
    freq = sine_freq[...] * (0.5 / math.pi)
    weight1[...] = jnp.zeros_like(weight1)
    weight1[0:feats, :] = embed_weight[...] * freq
    weight1[feats : feats + 1, :] = embed_bias[...] * freq
    weight2[...] = jnp.zeros_like(weight2)
    weight2[0:units, :] = mid_weight[...] * freq
    weight2[units : units + 1, :] = mid_bias[...] * freq
    hidden[...] = jnp.where(
        lax.broadcasted_iota(jnp.int32, hidden.shape, 0) == units, 1.0, 0.0
    )
    hidden[0:units, :] = sine_of_turns(dot_first(weight1[...], features))
    second = sine_of_turns(dot_first(weight2[...], hidden[...]))
    rate = decay[...]
    raw = dot_first(out_weight[...], second, 1)
    row = lax.broadcasted_iota(jnp.int32, (8, channels), 0)
    rates = jnp.broadcast_to(rate, row.shape)
    rates = jnp.where(row == 0, -rates, jnp.where(row == 1, 0.5 * jnp.log(2.0 * rates), 0.0))
    row = lax.broadcasted_iota(jnp.int32, (8, local_len), 0)
    times = jnp.where(row == 0, token[0:8, :].astype(jnp.float32), jnp.where(row == 1, 1.0, 0.0))
    filt = raw * jnp.exp(dot_first(rates, times))
    filt_high = filt.astype(jnp.bfloat16).astype(jnp.float32)

    for load in first_loads:
        load.wait()

    parts = (
        signal[...].astype(jnp.float32),
        in_gate[...].astype(jnp.float32),
        filt_high,
        filt - filt_high,
    )
    height = len(parts) * per_block
    for kind, part in enumerate(parts):
        for quarter in range(per_block):
            packed32[pl.ds(kind * per_block + quarter, channels, stride=height), :] = part[
                :, quarter * LANES : (quarter + 1) * LANES
            ]
    packed[...] = packed32[...].astype(jnp.bfloat16).reshape(packed.shape)

    @pl.when(owner)
    def _():
        pl.semaphore_wait(barrier, owners - 1)

    @pl.when(jnp.logical_not(owner))
    def _():
        pl.semaphore_wait(barrier, owners)

    def send(chip):
        pltpu.make_async_remote_copy(
            src_ref=packed.at[chip],
            dst_ref=arrived.at[me],
            send_sem=send_sem,
            recv_sem=recv_sem,
            device_id={"seq": chip * CORES},
            device_id_type=MESH,
        ).start()

    for chip, here in chips:
        if not here:
            send(chip)

    @pl.when(owner)
    def _():
        pltpu.make_async_copy(packed.at[mine], arrived.at[me], recv_sem).start()

    @pl.when(jnp.logical_not(owner))
    def _():
        send(mine)

    @pl.when(owner)
    def _():
        for load in owner_loads:
            load.wait()

        taps_row = jnp.broadcast_to(taps[pl.ds(mine, 1), :], (LANES, LANES))
        circulant = pltpu.roll(taps_row, 0, 1, stride=1, stride_axis=0)
        source = lax.broadcasted_iota(jnp.int32, (LANES, LANES), 0)
        target = lax.broadcasted_iota(jnp.int32, (LANES, LANES), 1)
        same = target >= source
        toeplitz = jnp.concatenate(
            [jnp.where(same, circulant, 0.0), jnp.where(same, 0.0, circulant)], axis=1
        )
        toeplitz = jnp.concatenate(split(toeplitz), axis=0)
        lane = lax.broadcasted_iota(jnp.int32, (1, channels), 1)
        gain = jnp.sum(jnp.where(lane == mine, skip[...], 0.0), axis=1, keepdims=True)
        pltpu.make_async_copy(arrived, arrived, recv_sem).wait()

        blocks = arrived[...].astype(jnp.float32).reshape(seq_devs // 2, 2, height, LANES)
        upper = lax.broadcasted_iota(jnp.int32, (seq_devs // 2, 8, LANES), 1) < per_block

        def unpack(pair):
            even = blocks[:, 0, 8 * pair : 8 * pair + 8, :]
            odd = blocks[:, 1, 8 * pair : 8 * pair + 8, :]
            one = jnp.where(upper, even, pltpu.roll(odd, 4, 1))
            two = jnp.where(upper, pltpu.roll(even, 4, 1), odd)
            return one.reshape(rows, LANES), two.reshape(rows, LANES)

        values, gates = unpack(0)
        filter_parts = [part.astype(jnp.bfloat16) for part in unpack(1)]
        values = values.astype(jnp.bfloat16)
        both = dot(jnp.concatenate([values, values], axis=1), toeplitz)
        later = pltpu.roll(both[:, LANES:], 1, 0)
        later = jnp.where(lax.broadcasted_iota(jnp.int32, later.shape, 0) == 0, 0.0, later)
        gated = gates * (both[:, :LANES] + later)

        gated_parts = split(gated)
        columns = [
            jnp.concatenate([g, f], axis=1) for g, f in zip(gated_parts, filter_parts)
        ]
        outer_cols = dot3((outer[0], outer[1]), columns)
        real, imag = outer_cols[:rows, :], outer_cols[rows:, :]
        cosine = jnp.concatenate([twiddle[0], twiddle[0]], axis=1)
        sine = jnp.concatenate([twiddle[1], twiddle[1]], axis=1)
        turned_real = real * cosine + imag * sine
        turned_imag = imag * cosine - real * sine

        def spectrum(lanes):
            joined = jnp.concatenate([turned_real[:, lanes], turned_imag[:, lanes]], axis=1)
            full = dot3(split(joined), (inner[0], inner[1]))
            return full[:, :LANES], full[:, LANES:]

        gated_real, gated_imag = spectrum(slice(0, LANES))
        filt_real, filt_imag = spectrum(slice(LANES, 2 * LANES))
        product = jnp.concatenate(
            [
                gated_real * filt_real - gated_imag * filt_imag,
                gated_real * filt_imag + gated_imag * filt_real,
            ],
            axis=1,
        )
        undone = dot3(split(product), (inner_back[0], inner_back[1]))
        real, imag = undone[:, :LANES], undone[:, LANES:]
        cosine, sine = twiddle[0], twiddle[1]
        stacked = jnp.concatenate(
            [real * cosine - imag * sine, imag * cosine + real * sine], axis=0
        )
        conv = dot3((back[0], back[1]), split(stacked))
        answer[...] = (conv + gain * gated).reshape(answer.shape)

        for chip, here in chips:
            for core in range(1 if here else 0, CORES):
                device = chip * CORES + core
                pltpu.make_async_remote_copy(
                    src_ref=answer.at[device],
                    dst_ref=answers.at[mine],
                    send_sem=back_send_sem,
                    recv_sem=back_recv_sem,
                    device_id={"seq": device},
                    device_id_type=MESH,
                ).start()
        pltpu.make_async_copy(answer.at[me], answers.at[mine], back_recv_sem).start()

    pltpu.make_async_copy(answers, answers, back_recv_sem).wait()
    for quarter in range(per_block):
        result[:, quarter * LANES : (quarter + 1) * LANES] = answers[:, quarter, :]

    @pl.when(owner)
    def _():
        sent = packed.at[0 : owners - 1]
        pltpu.make_async_copy(sent, sent, send_sem).wait()
        replied = answer.at[0 : seq_devs - 1]
        pltpu.make_async_copy(replied, replied, back_send_sem).wait()

    @pl.when(jnp.logical_not(owner))
    def _():
        pltpu.make_async_copy(packed, packed, send_sem).wait()


def on_device(
    consts,
    signal,
    in_gate,
    out_gate,
    short_taps,
    skip_gain,
    decay_rate,
    embed_weight,
    embed_bias,
    sine_freq,
    mid_weight,
    mid_bias,
    out_weight,
):
    channels, local_len = signal.shape
    seq_devs = lax.axis_size("seq")
    per_block = local_len // LANES
    units = mid_weight.shape[0]
    vmem = pl.BlockSpec(memory_space=pltpu.VMEM)
    operands = (
        signal,
        in_gate,
        short_taps,
        skip_gain[None, :],
        decay_rate[None, :],
        embed_weight,
        embed_bias[None, :],
        sine_freq[None, :],
        mid_weight,
        mid_bias[None, :],
        out_weight.T,
        *[jnp.asarray(const) for const in consts],
    )
    height1 = (embed_weight.shape[0] + 1 + 7) // 8 * 8
    height2 = (units + 1 + 7) // 8 * 8
    result = pl.pallas_call(
        functools.partial(kernel, seq_devs),
        out_shape=pltpu.VMEM((channels, local_len), jnp.float32),
        in_specs=[pl.BlockSpec(memory_space=pl.ANY)] * len(operands),
        out_specs=vmem,
        scratch_shapes=[
            *[pltpu.VMEM(operand.shape, operand.dtype) for operand in operands],
            pltpu.VMEM((height1, units), jnp.float32),
            pltpu.VMEM((height2, units), jnp.float32),
            pltpu.VMEM((height2, local_len), jnp.float32),
            pltpu.VMEM((channels * 4 * per_block, LANES), jnp.float32),
            pltpu.VMEM((channels, 4 * per_block, LANES), jnp.bfloat16),
            pltpu.VMEM((seq_devs, 4 * per_block, LANES), jnp.bfloat16),
            pltpu.VMEM((seq_devs, per_block, LANES), jnp.float32),
            pltpu.VMEM((channels, per_block, LANES), jnp.float32),
            pltpu.SemaphoreType.DMA((len(operands),)),
            pltpu.SemaphoreType.DMA,
            pltpu.SemaphoreType.DMA,
            pltpu.SemaphoreType.DMA,
            pltpu.SemaphoreType.DMA,
        ],
        compiler_params=pltpu.CompilerParams(collective_id=0, has_side_effects=True),
    )(*operands)
    return (out_gate.astype(jnp.float32) * result).astype(jnp.bfloat16)


def solution(mesh):
    consts = tables(32768)
    in_specs = (
        P("ch", "seq"),
        P("ch", "seq"),
        P("ch", "seq"),
        P("ch", None),
        P("ch"),
        P("ch"),
        P(),
        P(),
        P(),
        P(),
        P(),
        P(None, "ch"),
    )
    return jax.shard_map(
        functools.partial(on_device, consts),
        mesh=mesh,
        in_specs=in_specs,
        out_specs=P("ch", "seq"),
        check_vma=False,
    )
```

```python
import functools
import math

import jax
import jax.numpy as jnp
import ml_dtypes
import numpy as np
from jax import lax
from jax.experimental import pallas as pl
from jax.experimental.pallas import tpu as pltpu
from jax.sharding import PartitionSpec as P

MESH = pl.DeviceIdType.MESH
HIGHEST = lax.Precision.HIGHEST
LANES = 128
GRID = (4, 8)
CORES = 2
WORK_ROWS = 4
STAND_IN = GRID[1] * CORES - 1

SINE = (
    25.132741928100586,
    -64.83584594726562,
    67.07760620117188,
    -38.512542724609375,
    14.178224563598633,
    -3.618709087371826,
    0.6094773411750793,
)


def far_first():
    def hops(offset):
        return sum(min(step, size - step) for step, size in zip(offset, GRID))

    offsets = [(dx, dy) for dx in range(GRID[0]) for dy in range(GRID[1])]
    return sorted(offsets, key=hops, reverse=True)


def workers_far_first():
    def hops(place):
        dx, near = place
        return min(dx, GRID[0] - dx) + WORK_ROWS - near

    places = [(dx, near) for dx in range(GRID[0]) for near in range(WORK_ROWS)]
    return sorted(places, key=hops, reverse=True)


def halves(table):
    high = table.astype(ml_dtypes.bfloat16)
    low = (table - high.astype(np.float64)).astype(ml_dtypes.bfloat16)
    return high, low


def tables(full_len):
    rows = full_len // LANES
    rows2 = 2 * rows
    k1 = np.arange(rows)[:, None] + 0.5
    angle = 2.0 * np.pi * k1 * np.arange(rows)[None, :] / rows2
    outer = np.concatenate([np.cos(angle), -np.sin(angle)], axis=0)
    turn = 2.0 * np.pi * k1 * np.arange(LANES)[None, :] / (2 * full_len)
    twiddle = np.stack([np.cos(turn), np.sin(turn)]).astype(np.float32)
    angle = 2.0 * np.pi * (np.outer(np.arange(LANES), np.arange(LANES)) % LANES) / LANES
    inner = np.block([[np.cos(angle), -np.sin(angle)], [np.sin(angle), np.cos(angle)]])
    back = outer.T * (2.0 / (2 * full_len))
    return (
        np.stack(halves(outer)),
        np.stack(halves(inner)),
        np.stack(halves(inner.T)),
        np.stack(halves(back)),
        twiddle,
    )


def sine_of_turns(turns):
    turns = turns - jnp.round(turns)
    square = turns * turns
    total = jnp.full_like(square, SINE[-1])
    for coefficient in SINE[-2::-1]:
        total = total * square + coefficient
    return total * (turns * (0.25 - square))


def split(value):
    high = value.astype(jnp.bfloat16)
    return high, (value - high.astype(jnp.float32)).astype(jnp.bfloat16)


def dot(a, b):
    return jnp.dot(a, b, preferred_element_type=jnp.float32)


def dot3(a, b):
    return dot(a[0], b[0]) + dot(a[0], b[1]) + dot(a[1], b[0])


def dot_first(a, b, axis=0):
    return lax.dot_general(
        a, b, (((axis,), (0,)), ((), ())), precision=HIGHEST, preferred_element_type=jnp.float32
    )


def kernel(
    seq_devs,
    *refs,
):
    sources, refs = refs[:16], refs[16:]
    result, targets, refs = refs[0], refs[1:17], refs[17:]
    signal, in_gate, taps, skip, decay = targets[:5]
    embed_weight, embed_bias, sine_freq, mid_weight, mid_bias, out_weight = targets[5:11]
    outer, inner, inner_back, back, twiddle = targets[11:]
    weight1, weight2, hidden, packed32, packed_filter32 = refs[:5]
    packed, packed_filter, arrived, arrived_filter, answer, answers = refs[5:11]
    load_sem, send_sem, recv_sem, filter_send_sem, filter_recv_sem = refs[11:16]
    back_send_sem, back_recv_sem = refs[16:]
    channels, local_len = signal.shape
    units = mid_weight.shape[0]
    feats = embed_weight.shape[0]
    per_block = local_len // LANES
    full_len = seq_devs * local_len
    rows = full_len // LANES
    owners = channels
    share = full_len // owners
    me = lax.axis_index("seq")
    chip = me // CORES
    x, y = chip // GRID[1], chip % GRID[1]
    by_x = [(x + dx) % GRID[0] for dx in range(GRID[0])]
    by_y = [(y + dy) % GRID[1] for dy in range(GRID[1])]
    spare = me == STAND_IN
    worker = jnp.logical_or(jnp.logical_and(y < WORK_ROWS, me != 0), spare)
    mine = jnp.where(spare, 0, (x * WORK_ROWS + y) * CORES + me % CORES)
    others = [
        (by_x[dx] * GRID[1] + by_y[dy], dx == dy == 0) for dx, dy in far_first()
    ]
    upward = (y + 2) // WORK_ROWS % 2
    workers = []
    for dx, near in workers_far_first():
        row = upward * near + (1 - upward) * (WORK_ROWS - 1 - near)
        for core in range(CORES):
            device = (by_x[dx] * GRID[1] + row) * CORES + core
            device = jnp.where(device == 0, STAND_IN, device)
            workers.append((device, (by_x[dx] * WORK_ROWS + row) * CORES + core))

    barrier = pltpu.get_barrier_semaphore()
    loads = [
        pltpu.make_async_copy(source, target, load_sem.at[index])
        for index, (source, target) in enumerate(zip(sources, targets))
    ]
    first_loads, weight_loads, owner_loads = loads[:2], loads[4:11], loads[2:4] + loads[11:]

    @pl.when(worker)
    def _():
        for chip, here in others:
            for core in range(CORES):
                device = chip * CORES + core

                def greet(device=device):
                    pl.semaphore_signal(
                        barrier, inc=1, device_id={"seq": device}, device_id_type=MESH
                    )

                if here:
                    pl.when(device != me)(greet)
                else:
                    greet()

    for load in first_loads:
        load.start()

    @pl.when(worker)
    def _():
        for load in weight_loads + owner_loads:
            load.start()

    for load in first_loads:
        load.wait()

    def spread(target, parts):
        height = target.shape[0] // channels
        row = 0
        for part in parts:
            for begin in range(0, part.shape[1], LANES):
                target[pl.ds(row, channels, stride=height), :] = part[:, begin : begin + LANES]
                row += 1

    spread(packed32, (signal[...].astype(jnp.float32), in_gate[...].astype(jnp.float32)))
    packed[...] = packed32[...].astype(jnp.bfloat16).reshape(packed.shape)

    @pl.when(worker)
    def _():
        row = lax.broadcasted_iota(jnp.int32, weight1.shape[:1] + (share,), 0)
        token = mine * share + lax.broadcasted_iota(jnp.int32, row.shape, 1)
        band = jnp.clip((row - 1) // 2, 0, 15)
        phase = (token << band) & (full_len - 1)
        turns = phase.astype(jnp.float32) * (1.0 / full_len) + jnp.where(row % 2 == 1, 0.25, 0.0)
        place = token.astype(jnp.float32) * (1.0 / full_len)
        features = jnp.where(
            row == 0,
            place,
            jnp.where(row < feats, sine_of_turns(turns), jnp.where(row == feats, 1.0, 0.0)),
        )
        for load in weight_loads:
            load.wait()
        freq = sine_freq[...] * (0.5 / math.pi)
        weight1[...] = jnp.zeros_like(weight1)
        weight1[0:feats, :] = embed_weight[...] * freq
        weight1[feats : feats + 1, :] = embed_bias[...] * freq
        weight2[...] = jnp.zeros_like(weight2)
        weight2[0:units, :] = mid_weight[...] * freq
        weight2[units : units + 1, :] = mid_bias[...] * freq
        hidden[...] = jnp.where(
            lax.broadcasted_iota(jnp.int32, hidden.shape, 0) == units, 1.0, 0.0
        )
        hidden[0:units, :] = sine_of_turns(dot_first(weight1[...], features))
        second = sine_of_turns(dot_first(weight2[...], hidden[...]))
        rate = decay[...]
        raw = dot_first(out_weight[...], second, 1)
        row = lax.broadcasted_iota(jnp.int32, (8, channels), 0)
        rates = jnp.broadcast_to(rate, row.shape)
        rates = jnp.where(row == 0, -rates, jnp.where(row == 1, 0.5 * jnp.log(2.0 * rates), 0.0))
        row = lax.broadcasted_iota(jnp.int32, (8, share), 0)
        times = jnp.where(
            row == 0, token[0:8, :].astype(jnp.float32), jnp.where(row == 1, 1.0, 0.0)
        )
        filt = raw * jnp.exp(dot_first(rates, times))
        filt_high = filt.astype(jnp.bfloat16).astype(jnp.float32)
        spread(packed_filter32, (filt_high, filt - filt_high))
        packed_filter[...] = (
            packed_filter32[...].astype(jnp.bfloat16).reshape(packed_filter.shape)
        )
        pl.semaphore_wait(barrier, owners - 1)

    @pl.when(jnp.logical_not(worker))
    def _():
        pl.semaphore_wait(barrier, owners)

    for device, index in workers:

        def send(device=device, index=index):
            pltpu.make_async_remote_copy(
                src_ref=packed.at[index],
                dst_ref=arrived.at[me],
                send_sem=send_sem,
                recv_sem=recv_sem,
                device_id={"seq": device},
                device_id_type=MESH,
            ).start()

        pl.when(device != me)(send)

    @pl.when(worker)
    def _():
        pltpu.make_async_copy(packed.at[mine], arrived.at[me], recv_sem).start()
        for device, index in workers:

            def send(device=device, index=index):
                pltpu.make_async_remote_copy(
                    src_ref=packed_filter.at[index],
                    dst_ref=arrived_filter.at[mine],
                    send_sem=filter_send_sem,
                    recv_sem=filter_recv_sem,
                    device_id={"seq": device},
                    device_id_type=MESH,
                ).start()

            pl.when(device != me)(send)
        pltpu.make_async_copy(
            packed_filter.at[mine], arrived_filter.at[mine], filter_recv_sem
        ).start()

    @pl.when(worker)
    def _():
        for load in owner_loads:
            load.wait()

        taps_row = jnp.broadcast_to(taps[pl.ds(mine, 1), :], (LANES, LANES))
        circulant = pltpu.roll(taps_row, 0, 1, stride=1, stride_axis=0)
        source = lax.broadcasted_iota(jnp.int32, (LANES, LANES), 0)
        target = lax.broadcasted_iota(jnp.int32, (LANES, LANES), 1)
        same = target >= source
        toeplitz = jnp.concatenate(
            [jnp.where(same, circulant, 0.0), jnp.where(same, 0.0, circulant)], axis=1
        )
        toeplitz = jnp.concatenate(split(toeplitz), axis=0)
        lane = lax.broadcasted_iota(jnp.int32, (1, channels), 1)
        gain = jnp.sum(jnp.where(lane == mine, skip[...], 0.0), axis=1, keepdims=True)
        pltpu.make_async_copy(arrived, arrived, recv_sem).wait()

        blocks = arrived[...].astype(jnp.float32).reshape(seq_devs // 2, 2, 8, LANES)
        even, odd = blocks[:, 0], blocks[:, 1]
        upper = lax.broadcasted_iota(jnp.int32, even.shape, 1) < per_block
        values = jnp.where(upper, even, pltpu.roll(odd, 4, 1)).reshape(rows, LANES)
        gates = jnp.where(upper, pltpu.roll(even, 4, 1), odd).reshape(rows, LANES)
        values = values.astype(jnp.bfloat16)
        both = dot(jnp.concatenate([values, values], axis=1), toeplitz)
        later = pltpu.roll(both[:, LANES:], 1, 0)
        later = jnp.where(lax.broadcasted_iota(jnp.int32, later.shape, 0) == 0, 0.0, later)
        gated = gates * (both[:, :LANES] + later)

        gated_parts = split(gated)
        pltpu.make_async_copy(arrived_filter, arrived_filter, filter_recv_sem).wait()
        blocks = arrived_filter[...].astype(jnp.float32)
        filter_parts = [
            blocks[:, begin : begin + share // LANES].reshape(rows, LANES).astype(jnp.bfloat16)
            for begin in (0, share // LANES)
        ]
        columns = [
            jnp.concatenate([g, f], axis=1) for g, f in zip(gated_parts, filter_parts)
        ]
        outer_cols = dot3((outer[0], outer[1]), columns)
        real, imag = outer_cols[:rows, :], outer_cols[rows:, :]
        cosine = jnp.concatenate([twiddle[0], twiddle[0]], axis=1)
        sine = jnp.concatenate([twiddle[1], twiddle[1]], axis=1)
        turned_real = real * cosine + imag * sine
        turned_imag = imag * cosine - real * sine

        def spectrum(lanes):
            joined = jnp.concatenate([turned_real[:, lanes], turned_imag[:, lanes]], axis=1)
            full = dot3(split(joined), (inner[0], inner[1]))
            return full[:, :LANES], full[:, LANES:]

        gated_real, gated_imag = spectrum(slice(0, LANES))
        filt_real, filt_imag = spectrum(slice(LANES, 2 * LANES))
        product = jnp.concatenate(
            [
                gated_real * filt_real - gated_imag * filt_imag,
                gated_real * filt_imag + gated_imag * filt_real,
            ],
            axis=1,
        )
        undone = dot3(split(product), (inner_back[0], inner_back[1]))
        real, imag = undone[:, :LANES], undone[:, LANES:]
        cosine, sine = twiddle[0], twiddle[1]
        stacked = jnp.concatenate(
            [real * cosine - imag * sine, imag * cosine + real * sine], axis=0
        )
        conv = dot3((back[0], back[1]), split(stacked))
        answer[...] = (conv + gain * gated).reshape(answer.shape)

        for chip, here in others:
            for core in range(CORES):
                device = chip * CORES + core

                def reply(device=device):
                    pltpu.make_async_remote_copy(
                        src_ref=answer.at[device],
                        dst_ref=answers.at[mine],
                        send_sem=back_send_sem,
                        recv_sem=back_recv_sem,
                        device_id={"seq": device},
                        device_id_type=MESH,
                    ).start()

                if here:
                    pl.when(device != me)(reply)
                else:
                    reply()
        pltpu.make_async_copy(answer.at[me], answers.at[mine], back_recv_sem).start()

    pltpu.make_async_copy(answers, answers, back_recv_sem).wait()
    for quarter in range(per_block):
        result[:, quarter * LANES : (quarter + 1) * LANES] = answers[:, quarter, :]

    @pl.when(worker)
    def _():
        sent = packed.at[0 : owners - 1]
        pltpu.make_async_copy(sent, sent, send_sem).wait()
        sent = packed_filter.at[0 : owners - 1]
        pltpu.make_async_copy(sent, sent, filter_send_sem).wait()
        replied = answer.at[0 : seq_devs - 1]
        pltpu.make_async_copy(replied, replied, back_send_sem).wait()

    @pl.when(jnp.logical_not(worker))
    def _():
        pltpu.make_async_copy(packed, packed, send_sem).wait()


def on_device(
    consts,
    signal,
    in_gate,
    out_gate,
    short_taps,
    skip_gain,
    decay_rate,
    embed_weight,
    embed_bias,
    sine_freq,
    mid_weight,
    mid_bias,
    out_weight,
):
    channels, local_len = signal.shape
    seq_devs = lax.axis_size("seq")
    per_block = local_len // LANES
    share = seq_devs * local_len // channels
    units = mid_weight.shape[0]
    vmem = pl.BlockSpec(memory_space=pltpu.VMEM)
    operands = (
        signal,
        in_gate,
        short_taps,
        skip_gain[None, :],
        decay_rate[None, :],
        embed_weight,
        embed_bias[None, :],
        sine_freq[None, :],
        mid_weight,
        mid_bias[None, :],
        out_weight.T,
        *[jnp.asarray(const) for const in consts],
    )
    height1 = (embed_weight.shape[0] + 1 + 7) // 8 * 8
    height2 = (units + 1 + 7) // 8 * 8
    result = pl.pallas_call(
        functools.partial(kernel, seq_devs),
        out_shape=pltpu.VMEM((channels, local_len), jnp.float32),
        in_specs=[pl.BlockSpec(memory_space=pl.ANY)] * len(operands),
        out_specs=vmem,
        scratch_shapes=[
            *[pltpu.VMEM(operand.shape, operand.dtype) for operand in operands],
            pltpu.VMEM((height1, units), jnp.float32),
            pltpu.VMEM((height2, units), jnp.float32),
            pltpu.VMEM((height2, share), jnp.float32),
            pltpu.VMEM((channels * 2 * per_block, LANES), jnp.float32),
            pltpu.VMEM((channels * 2 * share // LANES, LANES), jnp.float32),
            pltpu.VMEM((channels, 2 * per_block, LANES), jnp.bfloat16),
            pltpu.VMEM((channels, 2 * share // LANES, LANES), jnp.bfloat16),
            pltpu.VMEM((seq_devs, 2 * per_block, LANES), jnp.bfloat16),
            pltpu.VMEM((channels, 2 * share // LANES, LANES), jnp.bfloat16),
            pltpu.VMEM((seq_devs, per_block, LANES), jnp.float32),
            pltpu.VMEM((channels, per_block, LANES), jnp.float32),
            pltpu.SemaphoreType.DMA((len(operands),)),
            pltpu.SemaphoreType.DMA,
            pltpu.SemaphoreType.DMA,
            pltpu.SemaphoreType.DMA,
            pltpu.SemaphoreType.DMA,
            pltpu.SemaphoreType.DMA,
            pltpu.SemaphoreType.DMA,
        ],
        compiler_params=pltpu.CompilerParams(collective_id=0, has_side_effects=True),
    )(*operands)
    return (out_gate.astype(jnp.float32) * result).astype(jnp.bfloat16)


def solution(mesh):
    consts = tables(32768)
    in_specs = (
        P("ch", "seq"),
        P("ch", "seq"),
        P("ch", "seq"),
        P("ch", None),
        P("ch"),
        P("ch"),
        P(),
        P(),
        P(),
        P(),
        P(),
        P(None, "ch"),
    )
    return jax.shard_map(
        functools.partial(on_device, consts),
        mesh=mesh,
        in_specs=in_specs,
        out_specs=P("ch", "seq"),
        check_vma=False,
    )
```

```python
import functools
import math

import jax
import jax.numpy as jnp
import ml_dtypes
import numpy as np
from jax import lax
from jax.experimental import pallas as pl
from jax.experimental.pallas import tpu as pltpu
from jax.sharding import PartitionSpec as P

MESH = pl.DeviceIdType.MESH
HIGHEST = lax.Precision.HIGHEST
LANES = 128
GRID = (4, 8)
CORES = 2
WORK_ROWS = 4
STAND_IN = GRID[1] * CORES - 1
FAR_X = (2, 1, 3, 0)
REPLY_ROWS = (0, 1, 6, 5, 7, 2, 4, 3)

SINE = (
    25.132741928100586,
    -64.83584594726562,
    67.07760620117188,
    -38.512542724609375,
    14.178224563598633,
    -3.618709087371826,
    0.6094773411750793,
)


def far_first():
    def hops(offset):
        return sum(min(step, size - step) for step, size in zip(offset, GRID))

    offsets = [(dx, dy) for dx in range(GRID[0]) for dy in range(GRID[1])]
    return sorted(offsets, key=hops, reverse=True)


def workers_far_first():
    def hops(place):
        dx, near = place
        return min(dx, GRID[0] - dx) + WORK_ROWS - near

    places = [(dx, near) for dx in range(GRID[0]) for near in range(WORK_ROWS)]
    return sorted(places, key=hops, reverse=True)


def halves(table):
    high = table.astype(ml_dtypes.bfloat16)
    low = (table - high.astype(np.float64)).astype(ml_dtypes.bfloat16)
    return high, low


def tables(full_len):
    rows = full_len // LANES
    rows2 = 2 * rows
    k1 = np.arange(rows)[:, None] + 0.5
    angle = 2.0 * np.pi * k1 * np.arange(rows)[None, :] / rows2
    outer = np.concatenate([np.cos(angle), -np.sin(angle)], axis=0)
    turn = 2.0 * np.pi * k1 * np.arange(LANES)[None, :] / (2 * full_len)
    twiddle = np.stack([np.cos(turn), np.sin(turn)]).astype(np.float32)
    angle = 2.0 * np.pi * (np.outer(np.arange(LANES), np.arange(LANES)) % LANES) / LANES
    inner = np.block([[np.cos(angle), -np.sin(angle)], [np.sin(angle), np.cos(angle)]])
    back = outer.T * (2.0 / (2 * full_len))
    return (
        np.stack(halves(outer)),
        np.stack(halves(inner)),
        np.stack(halves(inner.T)),
        np.stack(halves(back)),
        twiddle,
    )


def sine_of_turns(turns):
    turns = turns - jnp.round(turns)
    square = turns * turns
    total = jnp.full_like(square, SINE[-1])
    for coefficient in SINE[-2::-1]:
        total = total * square + coefficient
    return total * (turns * (0.25 - square))


def split(value):
    high = value.astype(jnp.bfloat16)
    return high, (value - high.astype(jnp.float32)).astype(jnp.bfloat16)


def dot(a, b):
    return jnp.dot(a, b, preferred_element_type=jnp.float32)


def dot3(a, b):
    return dot(a[0], b[0]) + dot(a[0], b[1]) + dot(a[1], b[0])


def dot3_narrow(a, b):
    both = dot(a[0], jnp.concatenate([b[0], b[1]], axis=1))
    return both[:, :LANES] + both[:, LANES:] + dot(a[1], b[0])


def dot_first(a, b, axis=0):
    return lax.dot_general(
        a, b, (((axis,), (0,)), ((), ())), precision=HIGHEST, preferred_element_type=jnp.float32
    )


def kernel(
    seq_devs,
    *refs,
):
    sources, refs = refs[:16], refs[16:]
    result, targets, refs = refs[0], refs[1:17], refs[17:]
    signal, in_gate, taps, skip, decay = targets[:5]
    embed_weight, embed_bias, sine_freq, mid_weight, mid_bias, out_weight = targets[5:11]
    outer, inner, inner_back, back, twiddle = targets[11:]
    weight1, weight2, hidden, packed32, packed_filter32 = refs[:5]
    packed, packed_filter, arrived, arrived_filter, answer, answers = refs[5:11]
    load_sem, send_sem, recv_sem, filter_send_sem, filter_recv_sem = refs[11:16]
    back_send_sem, back_recv_sem = refs[16:]
    channels, local_len = signal.shape
    units = mid_weight.shape[0]
    feats = embed_weight.shape[0]
    per_block = local_len // LANES
    full_len = seq_devs * local_len
    rows = full_len // LANES
    owners = channels
    share = full_len // owners
    me = lax.axis_index("seq")
    chip = me // CORES
    x, y = chip // GRID[1], chip % GRID[1]
    by_x = [(x + dx) % GRID[0] for dx in range(GRID[0])]
    by_y = [(y + dy) % GRID[1] for dy in range(GRID[1])]
    spare = me == STAND_IN
    worker = jnp.logical_or(jnp.logical_and(y < WORK_ROWS, me != 0), spare)
    mine = jnp.where(spare, 0, (x * WORK_ROWS + y) * CORES + me % CORES)
    others = [
        (by_x[dx] * GRID[1] + by_y[dy], dx == dy == 0) for dx, dy in far_first()
    ]
    upward = (y + 2) // WORK_ROWS % 2
    workers = []
    for dx, near in workers_far_first():
        row = upward * near + (1 - upward) * (WORK_ROWS - 1 - near)
        for core in range(CORES):
            device = (by_x[dx] * GRID[1] + row) * CORES + core
            device = jnp.where(device == 0, STAND_IN, device)
            workers.append((device, (by_x[dx] * WORK_ROWS + row) * CORES + core))

    barrier = pltpu.get_barrier_semaphore()
    loads = [
        pltpu.make_async_copy(source, target, load_sem.at[index])
        for index, (source, target) in enumerate(zip(sources, targets))
    ]
    first_loads, weight_loads, owner_loads = loads[:2], loads[4:11], loads[2:4] + loads[11:]

    @pl.when(worker)
    def _():
        for chip, here in others:
            for core in range(CORES):
                device = chip * CORES + core

                def greet(device=device):
                    pl.semaphore_signal(
                        barrier, inc=1, device_id={"seq": device}, device_id_type=MESH
                    )

                if here:
                    pl.when(device != me)(greet)
                else:
                    greet()

    for load in first_loads:
        load.start()

    @pl.when(worker)
    def _():
        for load in weight_loads + owner_loads:
            load.start()

    for load in first_loads:
        load.wait()

    def spread(target, parts):
        height = target.shape[0] // channels
        row = 0
        for part in parts:
            for begin in range(0, part.shape[1], LANES):
                target[pl.ds(row, channels, stride=height), :] = part[:, begin : begin + LANES]
                row += 1

    spread(packed32, (signal[...].astype(jnp.float32), in_gate[...].astype(jnp.float32)))
    packed[...] = packed32[...].astype(jnp.bfloat16).reshape(packed.shape)

    @pl.when(worker)
    def _():
        row = lax.broadcasted_iota(jnp.int32, weight1.shape[:1] + (share,), 0)
        token = mine * share + lax.broadcasted_iota(jnp.int32, row.shape, 1)
        band = jnp.clip((row - 1) // 2, 0, 15)
        phase = (token << band) & (full_len - 1)
        turns = phase.astype(jnp.float32) * (1.0 / full_len) + jnp.where(row % 2 == 1, 0.25, 0.0)
        place = token.astype(jnp.float32) * (1.0 / full_len)
        features = jnp.where(
            row == 0,
            place,
            jnp.where(row < feats, sine_of_turns(turns), jnp.where(row == feats, 1.0, 0.0)),
        )
        for load in weight_loads:
            load.wait()
        freq = sine_freq[...] * (0.5 / math.pi)
        weight1[...] = jnp.zeros_like(weight1)
        weight1[0:feats, :] = embed_weight[...] * freq
        weight1[feats : feats + 1, :] = embed_bias[...] * freq
        weight2[...] = jnp.zeros_like(weight2)
        weight2[0:units, :] = mid_weight[...] * freq
        weight2[units : units + 1, :] = mid_bias[...] * freq
        hidden[...] = jnp.where(
            lax.broadcasted_iota(jnp.int32, hidden.shape, 0) == units, 1.0, 0.0
        )
        hidden[0:units, :] = sine_of_turns(dot_first(weight1[...], features))
        second = sine_of_turns(dot_first(weight2[...], hidden[...]))
        rate = decay[...]
        raw = dot_first(out_weight[...], second, 1)
        row = lax.broadcasted_iota(jnp.int32, (8, channels), 0)
        rates = jnp.broadcast_to(rate, row.shape)
        rates = jnp.where(row == 0, -rates, jnp.where(row == 1, 0.5 * jnp.log(2.0 * rates), 0.0))
        row = lax.broadcasted_iota(jnp.int32, (8, share), 0)
        times = jnp.where(
            row == 0, token[0:8, :].astype(jnp.float32), jnp.where(row == 1, 1.0, 0.0)
        )
        filt = raw * jnp.exp(dot_first(rates, times))
        filt_high = filt.astype(jnp.bfloat16).astype(jnp.float32)
        spread(packed_filter32, (filt_high, filt - filt_high))
        packed_filter[...] = (
            packed_filter32[...].astype(jnp.bfloat16).reshape(packed_filter.shape)
        )
        pl.semaphore_wait(barrier, owners - 1)

    @pl.when(jnp.logical_not(worker))
    def _():
        pl.semaphore_wait(barrier, owners)

    for device, index in workers:

        def send(device=device, index=index):
            pltpu.make_async_remote_copy(
                src_ref=packed.at[index],
                dst_ref=arrived.at[me],
                send_sem=send_sem,
                recv_sem=recv_sem,
                device_id={"seq": device},
                device_id_type=MESH,
            ).start()

        pl.when(device != me)(send)

    @pl.when(worker)
    def _():
        pltpu.make_async_copy(packed.at[mine], arrived.at[me], recv_sem).start()
        for device, index in workers:

            def send(device=device, index=index):
                pltpu.make_async_remote_copy(
                    src_ref=packed_filter.at[index],
                    dst_ref=arrived_filter.at[mine],
                    send_sem=filter_send_sem,
                    recv_sem=filter_recv_sem,
                    device_id={"seq": device},
                    device_id_type=MESH,
                ).start()

            pl.when(device != me)(send)
        pltpu.make_async_copy(
            packed_filter.at[mine], arrived_filter.at[mine], filter_recv_sem
        ).start()

    @pl.when(worker)
    def _():
        for load in owner_loads:
            load.wait()

        taps_row = jnp.broadcast_to(taps[pl.ds(mine, 1), :], (LANES, LANES))
        circulant = pltpu.roll(taps_row, 0, 1, stride=1, stride_axis=0)
        source = lax.broadcasted_iota(jnp.int32, (LANES, LANES), 0)
        target = lax.broadcasted_iota(jnp.int32, (LANES, LANES), 1)
        same = target >= source
        toeplitz = jnp.concatenate(
            [jnp.where(same, circulant, 0.0), jnp.where(same, 0.0, circulant)], axis=1
        )
        toeplitz = jnp.concatenate(split(toeplitz), axis=0)
        lane = lax.broadcasted_iota(jnp.int32, (1, channels), 1)
        gain = jnp.sum(jnp.where(lane == mine, skip[...], 0.0), axis=1, keepdims=True)

        def spectrum(parts):
            outer_rows = dot3_narrow((outer[0], outer[1]), parts)
            real, imag = outer_rows[:rows, :], outer_rows[rows:, :]
            turned = jnp.concatenate(
                [real * twiddle[0] + imag * twiddle[1], imag * twiddle[0] - real * twiddle[1]],
                axis=1,
            )
            full = dot3(split(turned), (inner[0], inner[1]))
            return full[:, :LANES], full[:, LANES:]

        pltpu.make_async_copy(arrived, arrived, recv_sem).wait()
        blocks = arrived[...].astype(jnp.float32).reshape(seq_devs // 2, 2, 8, LANES)
        even, odd = blocks[:, 0], blocks[:, 1]
        upper = lax.broadcasted_iota(jnp.int32, even.shape, 1) < per_block
        values = jnp.where(upper, even, pltpu.roll(odd, 4, 1)).reshape(rows, LANES)
        gates = jnp.where(upper, pltpu.roll(even, 4, 1), odd).reshape(rows, LANES)
        values = values.astype(jnp.bfloat16)
        both = dot(jnp.concatenate([values, values], axis=1), toeplitz)
        later = pltpu.roll(both[:, LANES:], 1, 0)
        later = jnp.where(lax.broadcasted_iota(jnp.int32, later.shape, 0) == 0, 0.0, later)
        gated = gates * (both[:, :LANES] + later)

        gated_real, gated_imag = spectrum(split(gated))
        pltpu.make_async_copy(arrived_filter, arrived_filter, filter_recv_sem).wait()
        blocks = arrived_filter[...].astype(jnp.float32)
        filter_parts = [
            blocks[:, begin : begin + share // LANES].reshape(rows, LANES).astype(jnp.bfloat16)
            for begin in (0, share // LANES)
        ]
        filt_real, filt_imag = spectrum(filter_parts)
        product = jnp.concatenate(
            [
                gated_real * filt_real - gated_imag * filt_imag,
                gated_real * filt_imag + gated_imag * filt_real,
            ],
            axis=1,
        )
        undone = dot3(split(product), (inner_back[0], inner_back[1]))
        real, imag = undone[:, :LANES], undone[:, LANES:]
        cosine, sine = twiddle[0], twiddle[1]
        stacked = jnp.concatenate(
            [real * cosine - imag * sine, imag * cosine + real * sine], axis=0
        )
        conv = dot3_narrow((back[0], back[1]), split(stacked))
        answer[...] = (conv + gain * gated).reshape(answer.shape)

        for row in REPLY_ROWS:
            for dx in FAR_X:
                for core in range(CORES):
                    device = (by_x[dx] * GRID[1] + row) * CORES + core

                    def reply(device=device):
                        pltpu.make_async_remote_copy(
                            src_ref=answer.at[device],
                            dst_ref=answers.at[mine],
                            send_sem=back_send_sem,
                            recv_sem=back_recv_sem,
                            device_id={"seq": device},
                            device_id_type=MESH,
                        ).start()

                    if dx == 0:
                        pl.when(device != me)(reply)
                    else:
                        reply()
        pltpu.make_async_copy(answer.at[me], answers.at[mine], back_recv_sem).start()

    pltpu.make_async_copy(answers, answers, back_recv_sem).wait()
    for quarter in range(per_block):
        result[:, quarter * LANES : (quarter + 1) * LANES] = answers[:, quarter, :]

    @pl.when(worker)
    def _():
        sent = packed.at[0 : owners - 1]
        pltpu.make_async_copy(sent, sent, send_sem).wait()
        sent = packed_filter.at[0 : owners - 1]
        pltpu.make_async_copy(sent, sent, filter_send_sem).wait()
        replied = answer.at[0 : seq_devs - 1]
        pltpu.make_async_copy(replied, replied, back_send_sem).wait()

    @pl.when(jnp.logical_not(worker))
    def _():
        pltpu.make_async_copy(packed, packed, send_sem).wait()


def on_device(
    consts,
    signal,
    in_gate,
    out_gate,
    short_taps,
    skip_gain,
    decay_rate,
    embed_weight,
    embed_bias,
    sine_freq,
    mid_weight,
    mid_bias,
    out_weight,
):
    channels, local_len = signal.shape
    seq_devs = lax.axis_size("seq")
    per_block = local_len // LANES
    share = seq_devs * local_len // channels
    units = mid_weight.shape[0]
    vmem = pl.BlockSpec(memory_space=pltpu.VMEM)
    operands = (
        signal,
        in_gate,
        short_taps,
        skip_gain[None, :],
        decay_rate[None, :],
        embed_weight,
        embed_bias[None, :],
        sine_freq[None, :],
        mid_weight,
        mid_bias[None, :],
        out_weight.T,
        *[jnp.asarray(const) for const in consts],
    )
    height1 = (embed_weight.shape[0] + 1 + 7) // 8 * 8
    height2 = (units + 1 + 7) // 8 * 8
    result = pl.pallas_call(
        functools.partial(kernel, seq_devs),
        out_shape=pltpu.VMEM((channels, local_len), jnp.float32),
        in_specs=[pl.BlockSpec(memory_space=pl.ANY)] * len(operands),
        out_specs=vmem,
        scratch_shapes=[
            *[pltpu.VMEM(operand.shape, operand.dtype) for operand in operands],
            pltpu.VMEM((height1, units), jnp.float32),
            pltpu.VMEM((height2, units), jnp.float32),
            pltpu.VMEM((height2, share), jnp.float32),
            pltpu.VMEM((channels * 2 * per_block, LANES), jnp.float32),
            pltpu.VMEM((channels * 2 * share // LANES, LANES), jnp.float32),
            pltpu.VMEM((channels, 2 * per_block, LANES), jnp.bfloat16),
            pltpu.VMEM((channels, 2 * share // LANES, LANES), jnp.bfloat16),
            pltpu.VMEM((seq_devs, 2 * per_block, LANES), jnp.bfloat16),
            pltpu.VMEM((channels, 2 * share // LANES, LANES), jnp.bfloat16),
            pltpu.VMEM((seq_devs, per_block, LANES), jnp.float32),
            pltpu.VMEM((channels, per_block, LANES), jnp.float32),
            pltpu.SemaphoreType.DMA((len(operands),)),
            pltpu.SemaphoreType.DMA,
            pltpu.SemaphoreType.DMA,
            pltpu.SemaphoreType.DMA,
            pltpu.SemaphoreType.DMA,
            pltpu.SemaphoreType.DMA,
            pltpu.SemaphoreType.DMA,
        ],
        compiler_params=pltpu.CompilerParams(collective_id=0, has_side_effects=True),
    )(*operands)
    return (out_gate.astype(jnp.float32) * result).astype(jnp.bfloat16)


def solution(mesh):
    consts = tables(32768)
    in_specs = (
        P("ch", "seq"),
        P("ch", "seq"),
        P("ch", "seq"),
        P("ch", None),
        P("ch"),
        P("ch"),
        P(),
        P(),
        P(),
        P(),
        P(),
        P(None, "ch"),
    )
    return jax.shard_map(
        functools.partial(on_device, consts),
        mesh=mesh,
        in_specs=in_specs,
        out_specs=P("ch", "seq"),
        check_vma=False,
    )
```

```python
import functools
import math

import jax
import jax.numpy as jnp
import ml_dtypes
import numpy as np
from jax import lax
from jax.experimental import pallas as pl
from jax.experimental.pallas import tpu as pltpu
from jax.sharding import PartitionSpec as P

MESH = pl.DeviceIdType.MESH
HIGHEST = lax.Precision.HIGHEST
LANES = 128
GRID = (4, 8)
CORES = 2
WORK_ROWS = 4
STAND_IN = GRID[1] * CORES - 1
FAR_X = (2, 1, 3, 0)
REPLY_ROWS = (0, 1, 6, 5, 7, 2, 4, 3)

SINE = (
    25.132741928100586,
    -64.83584594726562,
    67.07760620117188,
    -38.512542724609375,
    14.178224563598633,
    -3.618709087371826,
    0.6094773411750793,
)


def far_first():
    def hops(offset):
        return sum(min(step, size - step) for step, size in zip(offset, GRID))

    offsets = [(dx, dy) for dx in range(GRID[0]) for dy in range(GRID[1])]
    return sorted(offsets, key=hops, reverse=True)


def workers_far_first():
    def hops(place):
        dx, near = place
        return min(dx, GRID[0] - dx) + WORK_ROWS - near

    places = [(dx, near) for dx in range(GRID[0]) for near in range(WORK_ROWS)]
    return sorted(places, key=hops, reverse=True)


def halves(table):
    high = table.astype(ml_dtypes.bfloat16)
    low = (table - high.astype(np.float64)).astype(ml_dtypes.bfloat16)
    return high, low


def tables(full_len):
    rows = full_len // LANES
    rows2 = 2 * rows
    k1 = np.arange(rows)[:, None] + 0.5
    angle = 2.0 * np.pi * k1 * np.arange(rows)[None, :] / rows2
    outer = np.concatenate([np.cos(angle), -np.sin(angle)], axis=0)
    turn = 2.0 * np.pi * k1 * np.arange(LANES)[None, :] / (2 * full_len)
    twiddle = np.stack([np.cos(turn), np.sin(turn)]).astype(np.float32)
    angle = 2.0 * np.pi * (np.outer(np.arange(LANES), np.arange(LANES)) % LANES) / LANES
    inner = np.block([[np.cos(angle), -np.sin(angle)], [np.sin(angle), np.cos(angle)]])
    back = outer.T * (2.0 / (2 * full_len))
    return (
        np.stack(halves(outer)),
        np.stack(halves(inner)),
        np.stack(halves(inner.T)),
        np.stack(halves(back)),
        twiddle,
    )


def sine_of_turns(turns):
    turns = turns - jnp.round(turns)
    square = turns * turns
    total = jnp.full_like(square, SINE[-1])
    for coefficient in SINE[-2::-1]:
        total = total * square + coefficient
    return total * (turns * (0.25 - square))


def split(value):
    high = value.astype(jnp.bfloat16)
    return high, (value - high.astype(jnp.float32)).astype(jnp.bfloat16)


def dot(a, b):
    return jnp.dot(a, b, preferred_element_type=jnp.float32)


def dot3(a, b):
    return dot(a[0], b[0]) + dot(a[0], b[1]) + dot(a[1], b[0])


def dot3_narrow(a, b):
    both = dot(a[0], jnp.concatenate([b[0], b[1]], axis=1))
    return both[:, :LANES] + both[:, LANES:] + dot(a[1], b[0])


def dot_first(a, b, axis=0):
    return lax.dot_general(
        a, b, (((axis,), (0,)), ((), ())), precision=HIGHEST, preferred_element_type=jnp.float32
    )


def kernel(
    seq_devs,
    *refs,
):
    sources, refs = refs[:16], refs[16:]
    result, targets, refs = refs[0], refs[1:17], refs[17:]
    signal, in_gate, taps, skip, decay = targets[:5]
    embed_weight, embed_bias, sine_freq, mid_weight, mid_bias, out_weight = targets[5:11]
    outer, inner, inner_back, back, twiddle = targets[11:]
    weight1, weight2, hidden, packed32, packed_filter32 = refs[:5]
    packed, packed_filter, arrived, arrived_filter, answer = refs[5:10]
    load_sem, send_sem, recv_sem, filter_send_sem, filter_recv_sem = refs[10:15]
    back_send_sem, back_recv_sem = refs[15:]
    channels, local_len = signal.shape
    units = mid_weight.shape[0]
    feats = embed_weight.shape[0]
    per_block = local_len // LANES
    full_len = seq_devs * local_len
    rows = full_len // LANES
    owners = channels
    share = full_len // owners
    me = lax.axis_index("seq")
    chip = me // CORES
    x, y = chip // GRID[1], chip % GRID[1]
    by_x = [(x + dx) % GRID[0] for dx in range(GRID[0])]
    by_y = [(y + dy) % GRID[1] for dy in range(GRID[1])]
    spare = me == STAND_IN
    worker = jnp.logical_or(jnp.logical_and(y < WORK_ROWS, me != 0), spare)
    mine = jnp.where(spare, 0, (x * WORK_ROWS + y) * CORES + me % CORES)
    others = [
        (by_x[dx] * GRID[1] + by_y[dy], dx == dy == 0) for dx, dy in far_first()
    ]
    upward = (y + 2) // WORK_ROWS % 2
    workers = []
    for dx, near in workers_far_first():
        row = upward * near + (1 - upward) * (WORK_ROWS - 1 - near)
        for core in range(CORES):
            device = (by_x[dx] * GRID[1] + row) * CORES + core
            device = jnp.where(device == 0, STAND_IN, device)
            workers.append((device, (by_x[dx] * WORK_ROWS + row) * CORES + core))

    barrier = pltpu.get_barrier_semaphore()
    loads = [
        pltpu.make_async_copy(source, target, load_sem.at[index])
        for index, (source, target) in enumerate(zip(sources, targets))
    ]
    first_loads, weight_loads, owner_loads = loads[:2], loads[4:11], loads[2:4] + loads[11:]

    @pl.when(worker)
    def _():
        for chip, here in others:
            for core in range(CORES):
                device = chip * CORES + core

                def greet(device=device):
                    pl.semaphore_signal(
                        barrier, inc=1, device_id={"seq": device}, device_id_type=MESH
                    )

                if here:
                    pl.when(device != me)(greet)
                else:
                    greet()

    for load in first_loads:
        load.start()

    @pl.when(worker)
    def _():
        for load in weight_loads + owner_loads:
            load.start()

    for load in first_loads:
        load.wait()

    def spread(target, parts):
        height = target.shape[0] // channels
        row = 0
        for part in parts:
            for begin in range(0, part.shape[1], LANES):
                target[pl.ds(row, channels, stride=height), :] = part[:, begin : begin + LANES]
                row += 1

    spread(packed32, (signal[...].astype(jnp.float32), in_gate[...].astype(jnp.float32)))
    packed[...] = packed32[...].astype(jnp.bfloat16).reshape(packed.shape)

    @pl.when(worker)
    def _():
        row = lax.broadcasted_iota(jnp.int32, weight1.shape[:1] + (share,), 0)
        token = mine * share + lax.broadcasted_iota(jnp.int32, row.shape, 1)
        band = jnp.clip((row - 1) // 2, 0, 15)
        phase = (token << band) & (full_len - 1)
        turns = phase.astype(jnp.float32) * (1.0 / full_len) + jnp.where(row % 2 == 1, 0.25, 0.0)
        place = token.astype(jnp.float32) * (1.0 / full_len)
        features = jnp.where(
            row == 0,
            place,
            jnp.where(row < feats, sine_of_turns(turns), jnp.where(row == feats, 1.0, 0.0)),
        )
        for load in weight_loads:
            load.wait()
        freq = sine_freq[...] * (0.5 / math.pi)
        weight1[...] = jnp.zeros_like(weight1)
        weight1[0:feats, :] = embed_weight[...] * freq
        weight1[feats : feats + 1, :] = embed_bias[...] * freq
        weight2[...] = jnp.zeros_like(weight2)
        weight2[0:units, :] = mid_weight[...] * freq
        weight2[units : units + 1, :] = mid_bias[...] * freq
        hidden[...] = jnp.where(
            lax.broadcasted_iota(jnp.int32, hidden.shape, 0) == units, 1.0, 0.0
        )
        hidden[0:units, :] = sine_of_turns(dot_first(weight1[...], features))
        second = sine_of_turns(dot_first(weight2[...], hidden[...]))
        rate = decay[...]
        raw = dot_first(out_weight[...], second, 1)
        row = lax.broadcasted_iota(jnp.int32, (8, channels), 0)
        rates = jnp.broadcast_to(rate, row.shape)
        rates = jnp.where(row == 0, -rates, jnp.where(row == 1, 0.5 * jnp.log(2.0 * rates), 0.0))
        row = lax.broadcasted_iota(jnp.int32, (8, share), 0)
        times = jnp.where(
            row == 0, token[0:8, :].astype(jnp.float32), jnp.where(row == 1, 1.0, 0.0)
        )
        filt = raw * jnp.exp(dot_first(rates, times))
        filt_high = filt.astype(jnp.bfloat16).astype(jnp.float32)
        spread(packed_filter32, (filt_high, filt - filt_high))
        packed_filter[...] = (
            packed_filter32[...].astype(jnp.bfloat16).reshape(packed_filter.shape)
        )
        pl.semaphore_wait(barrier, owners - 1)

    @pl.when(jnp.logical_not(worker))
    def _():
        pl.semaphore_wait(barrier, owners)

    for device, index in workers:

        def send(device=device, index=index):
            pltpu.make_async_remote_copy(
                src_ref=packed.at[index],
                dst_ref=arrived.at[me],
                send_sem=send_sem,
                recv_sem=recv_sem,
                device_id={"seq": device},
                device_id_type=MESH,
            ).start()

        pl.when(device != me)(send)

    @pl.when(worker)
    def _():
        pltpu.make_async_copy(packed.at[mine], arrived.at[me], recv_sem).start()
        for device, index in workers:

            def send(device=device, index=index):
                pltpu.make_async_remote_copy(
                    src_ref=packed_filter.at[index],
                    dst_ref=arrived_filter.at[mine],
                    send_sem=filter_send_sem,
                    recv_sem=filter_recv_sem,
                    device_id={"seq": device},
                    device_id_type=MESH,
                ).start()

            pl.when(device != me)(send)
        pltpu.make_async_copy(
            packed_filter.at[mine], arrived_filter.at[mine], filter_recv_sem
        ).start()

    @pl.when(worker)
    def _():
        for load in owner_loads:
            load.wait()

        taps_row = jnp.broadcast_to(taps[pl.ds(mine, 1), :], (LANES, LANES))
        circulant = pltpu.roll(taps_row, 0, 1, stride=1, stride_axis=0)
        source = lax.broadcasted_iota(jnp.int32, (LANES, LANES), 0)
        target = lax.broadcasted_iota(jnp.int32, (LANES, LANES), 1)
        same = target >= source
        toeplitz = jnp.concatenate(
            [jnp.where(same, circulant, 0.0), jnp.where(same, 0.0, circulant)], axis=1
        )
        toeplitz = jnp.concatenate(split(toeplitz), axis=0)
        lane = lax.broadcasted_iota(jnp.int32, (1, channels), 1)
        gain = jnp.sum(jnp.where(lane == mine, skip[...], 0.0), axis=1, keepdims=True)

        def spectrum(parts):
            outer_rows = dot3_narrow((outer[0], outer[1]), parts)
            real, imag = outer_rows[:rows, :], outer_rows[rows:, :]
            turned = jnp.concatenate(
                [real * twiddle[0] + imag * twiddle[1], imag * twiddle[0] - real * twiddle[1]],
                axis=1,
            )
            full = dot3(split(turned), (inner[0], inner[1]))
            return full[:, :LANES], full[:, LANES:]

        pltpu.make_async_copy(arrived, arrived, recv_sem).wait()
        blocks = arrived[...].astype(jnp.float32).reshape(seq_devs // 2, 2, 8, LANES)
        even, odd = blocks[:, 0], blocks[:, 1]
        upper = lax.broadcasted_iota(jnp.int32, even.shape, 1) < per_block
        values = jnp.where(upper, even, pltpu.roll(odd, 4, 1)).reshape(rows, LANES)
        gates = jnp.where(upper, pltpu.roll(even, 4, 1), odd).reshape(rows, LANES)
        values = values.astype(jnp.bfloat16)
        both = dot(jnp.concatenate([values, values], axis=1), toeplitz)
        later = pltpu.roll(both[:, LANES:], 1, 0)
        later = jnp.where(lax.broadcasted_iota(jnp.int32, later.shape, 0) == 0, 0.0, later)
        gated = gates * (both[:, :LANES] + later)

        gated_real, gated_imag = spectrum(split(gated))
        pltpu.make_async_copy(arrived_filter, arrived_filter, filter_recv_sem).wait()
        blocks = arrived_filter[...].astype(jnp.float32)
        filter_parts = [
            blocks[:, begin : begin + share // LANES].reshape(rows, LANES).astype(jnp.bfloat16)
            for begin in (0, share // LANES)
        ]
        filt_real, filt_imag = spectrum(filter_parts)
        product = jnp.concatenate(
            [
                gated_real * filt_real - gated_imag * filt_imag,
                gated_real * filt_imag + gated_imag * filt_real,
            ],
            axis=1,
        )
        undone = dot3(split(product), (inner_back[0], inner_back[1]))
        real, imag = undone[:, :LANES], undone[:, LANES:]
        cosine, sine = twiddle[0], twiddle[1]
        stacked = jnp.concatenate(
            [real * cosine - imag * sine, imag * cosine + real * sine], axis=0
        )
        conv = dot3_narrow((back[0], back[1]), split(stacked))
        answer[...] = (conv + gain * gated).reshape(answer.shape)

        for row in REPLY_ROWS:
            for dx in FAR_X:
                for core in range(CORES):
                    device = (by_x[dx] * GRID[1] + row) * CORES + core

                    def reply(device=device):
                        pltpu.make_async_remote_copy(
                            src_ref=answer.at[device],
                            dst_ref=result.at[mine],
                            send_sem=back_send_sem,
                            recv_sem=back_recv_sem,
                            device_id={"seq": device},
                            device_id_type=MESH,
                        ).start()

                    if dx == 0:
                        pl.when(device != me)(reply)
                    else:
                        reply()
        pltpu.make_async_copy(answer.at[me], result.at[mine], back_recv_sem).start()

    pltpu.make_async_copy(result, result, back_recv_sem).wait()

    @pl.when(worker)
    def _():
        sent = packed.at[0 : owners - 1]
        pltpu.make_async_copy(sent, sent, send_sem).wait()
        sent = packed_filter.at[0 : owners - 1]
        pltpu.make_async_copy(sent, sent, filter_send_sem).wait()
        replied = answer.at[0 : seq_devs - 1]
        pltpu.make_async_copy(replied, replied, back_send_sem).wait()

    @pl.when(jnp.logical_not(worker))
    def _():
        pltpu.make_async_copy(packed, packed, send_sem).wait()


def on_device(
    consts,
    signal,
    in_gate,
    out_gate,
    short_taps,
    skip_gain,
    decay_rate,
    embed_weight,
    embed_bias,
    sine_freq,
    mid_weight,
    mid_bias,
    out_weight,
):
    channels, local_len = signal.shape
    seq_devs = lax.axis_size("seq")
    per_block = local_len // LANES
    share = seq_devs * local_len // channels
    units = mid_weight.shape[0]
    vmem = pl.BlockSpec(memory_space=pltpu.VMEM)
    operands = (
        signal,
        in_gate,
        short_taps,
        skip_gain[None, :],
        decay_rate[None, :],
        embed_weight,
        embed_bias[None, :],
        sine_freq[None, :],
        mid_weight,
        mid_bias[None, :],
        out_weight.T,
        *[jnp.asarray(const) for const in consts],
    )
    height1 = (embed_weight.shape[0] + 1 + 7) // 8 * 8
    height2 = (units + 1 + 7) // 8 * 8
    result = pl.pallas_call(
        functools.partial(kernel, seq_devs),
        out_shape=pltpu.VMEM((channels, per_block, LANES), jnp.float32),
        in_specs=[pl.BlockSpec(memory_space=pl.ANY)] * len(operands),
        out_specs=vmem,
        scratch_shapes=[
            *[pltpu.VMEM(operand.shape, operand.dtype) for operand in operands],
            pltpu.VMEM((height1, units), jnp.float32),
            pltpu.VMEM((height2, units), jnp.float32),
            pltpu.VMEM((height2, share), jnp.float32),
            pltpu.VMEM((channels * 2 * per_block, LANES), jnp.float32),
            pltpu.VMEM((channels * 2 * share // LANES, LANES), jnp.float32),
            pltpu.VMEM((channels, 2 * per_block, LANES), jnp.bfloat16),
            pltpu.VMEM((channels, 2 * share // LANES, LANES), jnp.bfloat16),
            pltpu.VMEM((seq_devs, 2 * per_block, LANES), jnp.bfloat16),
            pltpu.VMEM((channels, 2 * share // LANES, LANES), jnp.bfloat16),
            pltpu.VMEM((seq_devs, per_block, LANES), jnp.float32),
            pltpu.SemaphoreType.DMA((len(operands),)),
            pltpu.SemaphoreType.DMA,
            pltpu.SemaphoreType.DMA,
            pltpu.SemaphoreType.DMA,
            pltpu.SemaphoreType.DMA,
            pltpu.SemaphoreType.DMA,
            pltpu.SemaphoreType.DMA,
        ],
        compiler_params=pltpu.CompilerParams(collective_id=0, has_side_effects=True),
    )(*operands)
    result = result.reshape(channels, local_len)
    return (out_gate.astype(jnp.float32) * result).astype(jnp.bfloat16)


def solution(mesh):
    consts = tables(32768)
    in_specs = (
        P("ch", "seq"),
        P("ch", "seq"),
        P("ch", "seq"),
        P("ch", None),
        P("ch"),
        P("ch"),
        P(),
        P(),
        P(),
        P(),
        P(),
        P(None, "ch"),
    )
    return jax.shard_map(
        functools.partial(on_device, consts),
        mesh=mesh,
        in_specs=in_specs,
        out_specs=P("ch", "seq"),
        check_vma=False,
    )
```

```python
import functools
import math

import jax
import jax.numpy as jnp
import ml_dtypes
import numpy as np
from jax import lax
from jax.experimental import pallas as pl
from jax.experimental.pallas import tpu as pltpu
from jax.sharding import PartitionSpec as P

MESH = pl.DeviceIdType.MESH
HIGHEST = lax.Precision.HIGHEST
LANES = 128
GRID = (4, 8)
CORES = 2
WORK_ROWS = 4
STAND_IN = GRID[1] * CORES - 1
FAR_X = (2, 1, 3, 0)
GREET_FIRST = 10
REPLY_ROWS = (0, 1, 6, 5, 7, 2, 4, 3)

SINE = (
    25.132741928100586,
    -64.83584594726562,
    67.07760620117188,
    -38.512542724609375,
    14.178224563598633,
    -3.618709087371826,
    0.6094773411750793,
)


def far_first():
    def hops(offset):
        return sum(min(step, size - step) for step, size in zip(offset, GRID))

    offsets = [(dx, dy) for dx in range(GRID[0]) for dy in range(GRID[1])]
    return sorted(offsets, key=hops, reverse=True)


def workers_far_first():
    def hops(place):
        dx, near = place
        return min(dx, GRID[0] - dx) + WORK_ROWS - near

    places = [(dx, near) for dx in range(GRID[0]) for near in range(WORK_ROWS)]
    return sorted(places, key=hops, reverse=True)


def halves(table):
    high = table.astype(ml_dtypes.bfloat16)
    low = (table - high.astype(np.float64)).astype(ml_dtypes.bfloat16)
    return high, low


def tables(full_len):
    rows = full_len // LANES
    rows2 = 2 * rows
    k1 = np.arange(rows)[:, None] + 0.5
    angle = 2.0 * np.pi * k1 * np.arange(rows)[None, :] / rows2
    outer = np.concatenate([np.cos(angle), -np.sin(angle)], axis=0)
    turn = 2.0 * np.pi * k1 * np.arange(LANES)[None, :] / (2 * full_len)
    twiddle = np.stack([np.cos(turn), np.sin(turn)]).astype(np.float32)
    angle = 2.0 * np.pi * (np.outer(np.arange(LANES), np.arange(LANES)) % LANES) / LANES
    inner = np.block([[np.cos(angle), -np.sin(angle)], [np.sin(angle), np.cos(angle)]])
    back = outer.T * (2.0 / (2 * full_len))
    return (
        np.stack(halves(outer)),
        np.stack(halves(inner)),
        np.stack(halves(inner.T)),
        np.stack(halves(back)),
        twiddle,
    )


def sine_of_turns(turns):
    turns = turns - jnp.round(turns)
    square = turns * turns
    total = jnp.full_like(square, SINE[-1])
    for coefficient in SINE[-2::-1]:
        total = total * square + coefficient
    return total * (turns * (0.25 - square))


def split(value):
    high = value.astype(jnp.bfloat16)
    return high, (value - high.astype(jnp.float32)).astype(jnp.bfloat16)


def dot(a, b):
    return jnp.dot(a, b, preferred_element_type=jnp.float32)


def dot3(a, b):
    return dot(a[0], b[0]) + dot(a[0], b[1]) + dot(a[1], b[0])


def dot3_narrow(a, b):
    both = dot(a[0], jnp.concatenate([b[0], b[1]], axis=1))
    return both[:, :LANES] + both[:, LANES:] + dot(a[1], b[0])


def dot_first(a, b, axis=0):
    return lax.dot_general(
        a, b, (((axis,), (0,)), ((), ())), precision=HIGHEST, preferred_element_type=jnp.float32
    )


def kernel(
    seq_devs,
    *refs,
):
    sources, refs = refs[:16], refs[16:]
    result, targets, refs = refs[0], refs[1:17], refs[17:]
    signal, in_gate, taps, skip, decay = targets[:5]
    embed_weight, embed_bias, sine_freq, mid_weight, mid_bias, out_weight = targets[5:11]
    outer, inner, inner_back, back, twiddle = targets[11:]
    weight1, weight2, hidden, packed32, packed_filter32 = refs[:5]
    packed, packed_filter, arrived, arrived_filter, answer = refs[5:10]
    load_sem, send_sem, recv_sem, filter_send_sem, filter_recv_sem = refs[10:15]
    back_send_sem, back_recv_sem = refs[15:]
    channels, local_len = signal.shape
    units = mid_weight.shape[0]
    feats = embed_weight.shape[0]
    per_block = local_len // LANES
    full_len = seq_devs * local_len
    rows = full_len // LANES
    owners = channels
    share = full_len // owners
    me = lax.axis_index("seq")
    chip = me // CORES
    x, y = chip // GRID[1], chip % GRID[1]
    by_x = [(x + dx) % GRID[0] for dx in range(GRID[0])]
    by_y = [(y + dy) % GRID[1] for dy in range(GRID[1])]
    spare = me == STAND_IN
    worker = jnp.logical_or(jnp.logical_and(y < WORK_ROWS, me != 0), spare)
    mine = jnp.where(spare, 0, (x * WORK_ROWS + y) * CORES + me % CORES)
    others = [
        (by_x[dx] * GRID[1] + by_y[dy], dx == dy == 0) for dx, dy in far_first()
    ]
    upward = (y + 2) // WORK_ROWS % 2
    workers = []
    for dx, near in workers_far_first():
        row = upward * near + (1 - upward) * (WORK_ROWS - 1 - near)
        for core in range(CORES):
            device = (by_x[dx] * GRID[1] + row) * CORES + core
            device = jnp.where(device == 0, STAND_IN, device)
            workers.append((device, (by_x[dx] * WORK_ROWS + row) * CORES + core, dx == 0))

    barrier = pltpu.get_barrier_semaphore()
    loads = [
        pltpu.make_async_copy(source, target, load_sem.at[index])
        for index, (source, target) in enumerate(zip(sources, targets))
    ]
    first_loads, weight_loads, owner_loads = loads[:2], loads[4:11], loads[2:4] + loads[11:]

    def greet(device):
        pl.semaphore_signal(barrier, inc=1, device_id={"seq": device}, device_id_type=MESH)

    @pl.when(worker)
    def _():
        for chip, here in others[:GREET_FIRST]:
            for core in range(CORES):
                greet(chip * CORES + core)
        for load in weight_loads + first_loads:
            load.start()
        for chip, here in others[GREET_FIRST:]:
            for core in range(CORES):
                device = chip * CORES + core
                if here:
                    pl.when(device != me)(functools.partial(greet, device))
                else:
                    greet(device)
        for load in owner_loads:
            load.start()

    @pl.when(jnp.logical_not(worker))
    def _():
        for load in first_loads:
            load.start()

    for load in first_loads:
        load.wait()

    def spread(target, parts):
        height = target.shape[0] // channels
        row = 0
        for part in parts:
            for begin in range(0, part.shape[1], LANES):
                target[pl.ds(row, channels, stride=height), :] = part[:, begin : begin + LANES]
                row += 1

    spread(packed32, (signal[...].astype(jnp.float32), in_gate[...].astype(jnp.float32)))
    packed[...] = packed32[...].astype(jnp.bfloat16).reshape(packed.shape)

    @pl.when(worker)
    def _():
        row = lax.broadcasted_iota(jnp.int32, weight1.shape[:1] + (share,), 0)
        token = mine * share + lax.broadcasted_iota(jnp.int32, row.shape, 1)
        band = jnp.clip((row - 1) // 2, 0, 15)
        phase = (token << band) & (full_len - 1)
        turns = phase.astype(jnp.float32) * (1.0 / full_len) + jnp.where(row % 2 == 1, 0.25, 0.0)
        place = token.astype(jnp.float32) * (1.0 / full_len)
        features = jnp.where(
            row == 0,
            place,
            jnp.where(row < feats, sine_of_turns(turns), jnp.where(row == feats, 1.0, 0.0)),
        )
        for load in weight_loads:
            load.wait()
        freq = sine_freq[...] * (0.5 / math.pi)
        weight1[...] = jnp.zeros_like(weight1)
        weight1[0:feats, :] = embed_weight[...] * freq
        weight1[feats : feats + 1, :] = embed_bias[...] * freq
        weight2[...] = jnp.zeros_like(weight2)
        weight2[0:units, :] = mid_weight[...] * freq
        weight2[units : units + 1, :] = mid_bias[...] * freq
        hidden[...] = jnp.where(
            lax.broadcasted_iota(jnp.int32, hidden.shape, 0) == units, 1.0, 0.0
        )
        hidden[0:units, :] = sine_of_turns(dot_first(weight1[...], features))
        second = sine_of_turns(dot_first(weight2[...], hidden[...]))
        rate = decay[...]
        raw = dot_first(out_weight[...], second, 1)
        row = lax.broadcasted_iota(jnp.int32, (8, channels), 0)
        rates = jnp.broadcast_to(rate, row.shape)
        rates = jnp.where(row == 0, -rates, jnp.where(row == 1, 0.5 * jnp.log(2.0 * rates), 0.0))
        row = lax.broadcasted_iota(jnp.int32, (8, share), 0)
        times = jnp.where(
            row == 0, token[0:8, :].astype(jnp.float32), jnp.where(row == 1, 1.0, 0.0)
        )
        filt = raw * jnp.exp(dot_first(rates, times))
        filt_high = filt.astype(jnp.bfloat16).astype(jnp.float32)
        spread(packed_filter32, (filt_high, filt - filt_high))
        packed_filter[...] = (
            packed_filter32[...].astype(jnp.bfloat16).reshape(packed_filter.shape)
        )
        pl.semaphore_wait(barrier, owners - 1)

    @pl.when(jnp.logical_not(worker))
    def _():
        pl.semaphore_wait(barrier, owners)

    for device, index, near in workers:

        def send(device=device, index=index):
            pltpu.make_async_remote_copy(
                src_ref=packed.at[index],
                dst_ref=arrived.at[me],
                send_sem=send_sem,
                recv_sem=recv_sem,
                device_id={"seq": device},
                device_id_type=MESH,
            ).start()

        pl.when(device != me)(send) if near else send()

    @pl.when(worker)
    def _():
        pltpu.make_async_copy(packed.at[mine], arrived.at[me], recv_sem).start()
        for device, index, near in workers:

            def send(device=device, index=index):
                pltpu.make_async_remote_copy(
                    src_ref=packed_filter.at[index],
                    dst_ref=arrived_filter.at[mine],
                    send_sem=filter_send_sem,
                    recv_sem=filter_recv_sem,
                    device_id={"seq": device},
                    device_id_type=MESH,
                ).start()

            pl.when(device != me)(send) if near else send()
        pltpu.make_async_copy(
            packed_filter.at[mine], arrived_filter.at[mine], filter_recv_sem
        ).start()

    @pl.when(worker)
    def _():
        for load in owner_loads:
            load.wait()

        taps_row = jnp.broadcast_to(taps[pl.ds(mine, 1), :], (LANES, LANES))
        circulant = pltpu.roll(taps_row, 0, 1, stride=1, stride_axis=0)
        source = lax.broadcasted_iota(jnp.int32, (LANES, LANES), 0)
        target = lax.broadcasted_iota(jnp.int32, (LANES, LANES), 1)
        same = target >= source
        toeplitz = jnp.concatenate(
            [jnp.where(same, circulant, 0.0), jnp.where(same, 0.0, circulant)], axis=1
        )
        toeplitz = jnp.concatenate(split(toeplitz), axis=0)
        lane = lax.broadcasted_iota(jnp.int32, (1, channels), 1)
        gain = jnp.sum(jnp.where(lane == mine, skip[...], 0.0), axis=1, keepdims=True)

        def spectrum(parts):
            outer_rows = dot3_narrow((outer[0], outer[1]), parts)
            real, imag = outer_rows[:rows, :], outer_rows[rows:, :]
            turned = jnp.concatenate(
                [real * twiddle[0] + imag * twiddle[1], imag * twiddle[0] - real * twiddle[1]],
                axis=1,
            )
            full = dot3(split(turned), (inner[0], inner[1]))
            return full[:, :LANES], full[:, LANES:]

        pltpu.make_async_copy(arrived, arrived, recv_sem).wait()
        blocks = arrived[...].astype(jnp.float32).reshape(seq_devs // 2, 2, 8, LANES)
        even, odd = blocks[:, 0], blocks[:, 1]
        upper = lax.broadcasted_iota(jnp.int32, even.shape, 1) < per_block
        values = jnp.where(upper, even, pltpu.roll(odd, 4, 1)).reshape(rows, LANES)
        gates = jnp.where(upper, pltpu.roll(even, 4, 1), odd).reshape(rows, LANES)
        values = values.astype(jnp.bfloat16)
        both = dot(jnp.concatenate([values, values], axis=1), toeplitz)
        later = pltpu.roll(both[:, LANES:], 1, 0)
        later = jnp.where(lax.broadcasted_iota(jnp.int32, later.shape, 0) == 0, 0.0, later)
        gated = gates * (both[:, :LANES] + later)

        gated_real, gated_imag = spectrum(split(gated))
        pltpu.make_async_copy(arrived_filter, arrived_filter, filter_recv_sem).wait()
        blocks = arrived_filter[...].astype(jnp.float32)
        filter_parts = [
            blocks[:, begin : begin + share // LANES].reshape(rows, LANES).astype(jnp.bfloat16)
            for begin in (0, share // LANES)
        ]
        filt_real, filt_imag = spectrum(filter_parts)
        product = jnp.concatenate(
            [
                gated_real * filt_real - gated_imag * filt_imag,
                gated_real * filt_imag + gated_imag * filt_real,
            ],
            axis=1,
        )
        undone = dot3(split(product), (inner_back[0], inner_back[1]))
        real, imag = undone[:, :LANES], undone[:, LANES:]
        cosine, sine = twiddle[0], twiddle[1]
        stacked = jnp.concatenate(
            [real * cosine - imag * sine, imag * cosine + real * sine], axis=0
        )
        conv = dot3_narrow((back[0], back[1]), split(stacked))
        answer[...] = (conv + gain * gated).reshape(answer.shape)

        for row in REPLY_ROWS:
            for dx in FAR_X:
                for core in range(CORES):
                    device = (by_x[dx] * GRID[1] + row) * CORES + core

                    def reply(device=device):
                        pltpu.make_async_remote_copy(
                            src_ref=answer.at[device],
                            dst_ref=result.at[mine],
                            send_sem=back_send_sem,
                            recv_sem=back_recv_sem,
                            device_id={"seq": device},
                            device_id_type=MESH,
                        ).start()

                    if dx == 0:
                        pl.when(device != me)(reply)
                    else:
                        reply()
        pltpu.make_async_copy(answer.at[me], result.at[mine], back_recv_sem).start()

    pltpu.make_async_copy(result, result, back_recv_sem).wait()

    @pl.when(worker)
    def _():
        sent = packed.at[0 : owners - 1]
        pltpu.make_async_copy(sent, sent, send_sem).wait()
        sent = packed_filter.at[0 : owners - 1]
        pltpu.make_async_copy(sent, sent, filter_send_sem).wait()
        replied = answer.at[0 : seq_devs - 1]
        pltpu.make_async_copy(replied, replied, back_send_sem).wait()

    @pl.when(jnp.logical_not(worker))
    def _():
        pltpu.make_async_copy(packed, packed, send_sem).wait()


def on_device(
    consts,
    signal,
    in_gate,
    out_gate,
    short_taps,
    skip_gain,
    decay_rate,
    embed_weight,
    embed_bias,
    sine_freq,
    mid_weight,
    mid_bias,
    out_weight,
):
    channels, local_len = signal.shape
    seq_devs = lax.axis_size("seq")
    per_block = local_len // LANES
    share = seq_devs * local_len // channels
    units = mid_weight.shape[0]
    vmem = pl.BlockSpec(memory_space=pltpu.VMEM)
    operands = (
        signal,
        in_gate,
        short_taps,
        skip_gain[None, :],
        decay_rate[None, :],
        embed_weight,
        embed_bias[None, :],
        sine_freq[None, :],
        mid_weight,
        mid_bias[None, :],
        out_weight.T,
        *[jnp.asarray(const) for const in consts],
    )
    height1 = (embed_weight.shape[0] + 1 + 7) // 8 * 8
    height2 = (units + 1 + 7) // 8 * 8
    result = pl.pallas_call(
        functools.partial(kernel, seq_devs),
        out_shape=pltpu.VMEM((channels, per_block, LANES), jnp.float32),
        in_specs=[pl.BlockSpec(memory_space=pl.ANY)] * len(operands),
        out_specs=vmem,
        scratch_shapes=[
            *[pltpu.VMEM(operand.shape, operand.dtype) for operand in operands],
            pltpu.VMEM((height1, units), jnp.float32),
            pltpu.VMEM((height2, units), jnp.float32),
            pltpu.VMEM((height2, share), jnp.float32),
            pltpu.VMEM((channels * 2 * per_block, LANES), jnp.float32),
            pltpu.VMEM((channels * 2 * share // LANES, LANES), jnp.float32),
            pltpu.VMEM((channels, 2 * per_block, LANES), jnp.bfloat16),
            pltpu.VMEM((channels, 2 * share // LANES, LANES), jnp.bfloat16),
            pltpu.VMEM((seq_devs, 2 * per_block, LANES), jnp.bfloat16),
            pltpu.VMEM((channels, 2 * share // LANES, LANES), jnp.bfloat16),
            pltpu.VMEM((seq_devs, per_block, LANES), jnp.float32),
            pltpu.SemaphoreType.DMA((len(operands),)),
            pltpu.SemaphoreType.DMA,
            pltpu.SemaphoreType.DMA,
            pltpu.SemaphoreType.DMA,
            pltpu.SemaphoreType.DMA,
            pltpu.SemaphoreType.DMA,
            pltpu.SemaphoreType.DMA,
        ],
        compiler_params=pltpu.CompilerParams(collective_id=0, has_side_effects=True),
    )(*operands)
    result = result.reshape(channels, local_len)
    return (out_gate.astype(jnp.float32) * result).astype(jnp.bfloat16)


def solution(mesh):
    consts = tables(32768)
    in_specs = (
        P("ch", "seq"),
        P("ch", "seq"),
        P("ch", "seq"),
        P("ch", None),
        P("ch"),
        P("ch"),
        P(),
        P(),
        P(),
        P(),
        P(),
        P(None, "ch"),
    )
    return jax.shard_map(
        functools.partial(on_device, consts),
        mesh=mesh,
        in_specs=in_specs,
        out_specs=P("ch", "seq"),
        check_vma=False,
    )
```
